32 devices in a mesh: grp: 2 (over x), pop: 16 (over z, y, core).
Axes of the slice: x: 2, y: 2, z: 4, core: 2. Of those that a mesh axis runs over, the one named last changes fastest.
Arguments:
- inputs: bfloat16 [64, 5120], P('grp'), parts along dimension 0, may hold values from -6 to 6
- gate_weight: bfloat16 [5120, 13824], P(None, 'pop'), may hold values from -0.078125 to 0.078125
- up_weight: bfloat16 [5120, 13824], P(None, 'pop'), may hold values from -0.078125 to 0.078125
- member_seeds: int32 [128], P(('grp', 'pop')), parts along dimension 0, may hold values from 0 to 1048575
- member_ranks: int32 [128], P(('grp', 'pop')), parts along dimension 0, may hold values from 0 to 63, each once
Outputs:
- hidden: bfloat16 [128, 32, 13824], P(('grp', 'pop')), parts along dimension 0
- gate_update: bfloat16 [10240, 13824], P('grp', 'pop'), parts along dimension 0
- up_update: bfloat16 [10240, 13824], P('grp', 'pop'), parts along dimension 0
The draws below stay inside these ranges and needn't reach their ends.
There are 2 independent parts, one for each index of `grp`. The reference program is written for one: setup_inputs(seed, part) draws one part's arguments, and reference() takes and returns one part's arrays. A program takes and returns all parts, laid end to end along the dimension named above; an argument that names none is the same for every part. Nothing has to cross between parts.
Inputs may be any that keep to these rules, and one draw needn't show every extreme that they name: member_ranks holds each number from 0 to 63 once.
All inputs are finite; a program needn't handle non-finite values.
Results may differ from the reference program's by a relative error of at most 0.012.
Values may be sent and summed in bfloat16 or wider, within the bound.
No kernel may reach another device: no remote copies, remote signals or barrier semaphores. Data moves between devices by JAX's collectives and lax.ppermute only.
A program may use at most 128 MiB of HBM per device.

```python
import math
import jax
import jax.numpy as jnp
from jax import lax

D = 5120
FF = 13824
R = 4
SEQ = 32
POP = 64


def plant(entries, own_key, low, high):
    shape = entries.shape
    index_at = [jax.random.randint(jax.random.fold_in(own_key, axis), (), 0, shape[axis]) for axis in range(len(shape))]
    entries = entries.at[tuple(index_at)].set(low)
    longest = shape.index(max(shape))
    index_at[longest] = (index_at[longest] + 1) % shape[longest]
    return entries.at[tuple(index_at)].set(high)


def block_levels(rng, extent, cuts, least, high):
    factor_of = 1.0
    for dim, blocks in cuts:
        draws = jax.random.uniform(jax.random.fold_in(jax.random.fold_in(rng, 6), dim), (blocks,), jnp.float32, least / len(cuts), high / len(cuts))
        factor_of = factor_of * jnp.repeat(jnp.exp(draws), extent[dim] // blocks).reshape((-1,) + (1,) * (len(extent) - 1 - dim))
    return factor_of


def normal_values(own_key, extent, deviation, reach, split=(), kind=jnp.bfloat16):
    values = jax.random.normal(own_key, extent, jnp.float32) * deviation
    if len(split) > 0:
        values = block_levels(own_key, extent, split, -0.22, 0.18) * values
    return jnp.clip(values, min=-reach, max=reach).astype(kind)


def setup_inputs(seed: int = 0, part: int = 0) -> dict:
    splits = jax.random.split(jax.random.key(seed), 6)
    part_splits = jax.random.split(jax.random.fold_in(splits[5], part), 6)
    inputs = normal_values(part_splits[0], (SEQ, D), 1.0, 6.0)
    gate_weight = normal_values(splits[1], (D, FF), D ** -0.5, 0.078125, ((1, 16),))
    up_weight = normal_values(splits[2], (D, FF), D ** -0.5, 0.078125, ((1, 16),))
    member_seeds = plant(jax.random.randint(part_splits[3], (POP,), 0, 1048576), jax.random.fold_in(part_splits[3], 1), 0, 1048575).astype(jnp.int32)
    member_ranks = jax.random.permutation(part_splits[4], POP).astype(jnp.int32)
    return dict(inputs=inputs, gate_weight=gate_weight, up_weight=up_weight, member_seeds=member_seeds, member_ranks=member_ranks)


hash_multiplier = 73244475
NOISE_SCALE = math.sqrt(3.0) / 32768.0
PERTURB = 0.3

def scramble(value):
    value = (value ^ value >> 16 & 65535) * hash_multiplier
    value = (value ^ value >> 16 & 65535) * hash_multiplier
    return value ^ value >> 16 & 65535

def factor(member_seeds, stream, offset, length):
    slots = jnp.arange(R, dtype=jnp.int32)
    columns = offset + jnp.arange(length, dtype=jnp.int32)
    entry_index = columns[None, :] * R + slots[:, None]
    seed_keys = scramble(member_seeds * 4 + stream)
    hashed = scramble(seed_keys[:, None, None] ^ scramble(entry_index + 1)[None, :, :])
    centered = (hashed & 65535).astype(jnp.float32) - 32767.5
    return (centered * NOISE_SCALE).astype(jnp.bfloat16).reshape(member_seeds.shape[0] * R, length)

def shaped(member_ranks, population):
    return (member_ranks.astype(jnp.float32) + 0.5) / population - 0.5

def reference(inputs, gate_weight, up_weight, member_seeds, member_ranks):
    population = member_seeds.shape[0]
    fitness = shaped(member_ranks, population)
    lift = PERTURB / math.sqrt(R)
    norm_factor = 1.0 / math.sqrt(population * R)
    gate_in = factor(member_seeds, 0, 0, D)
    up_in = factor(member_seeds, 2, 0, D)
    gate_out = factor(member_seeds, 1, 0, FF)
    up_out = factor(member_seeds, 3, 0, FF)
    gate_coeff = (jnp.dot(inputs, gate_in.T, preferred_element_type=jnp.float32) / math.sqrt(D)).astype(jnp.bfloat16)
    up_coeff = (jnp.dot(inputs, up_in.T, preferred_element_type=jnp.float32) / math.sqrt(D)).astype(jnp.bfloat16)
    base_gate = jnp.dot(inputs, gate_weight, preferred_element_type=jnp.float32)
    base_up = jnp.dot(inputs, up_weight, preferred_element_type=jnp.float32)

    def member(pieces):
        gate_piece, up_piece, gate_rows, up_rows = pieces
        gate_total = base_gate + lift * jnp.dot(gate_piece, gate_rows, preferred_element_type=jnp.float32)
        up_total = base_up + lift * jnp.dot(up_piece, up_rows, preferred_element_type=jnp.float32)
        return (jax.nn.silu(gate_total) * up_total).astype(jnp.bfloat16)
    seq_len = inputs.shape[0]
    gate_members = gate_coeff.reshape(seq_len, population, R).transpose(1, 0, 2)
    up_members = up_coeff.reshape(seq_len, population, R).transpose(1, 0, 2)
    hidden = lax.map(member, (gate_members, up_members, gate_out.reshape(population, R, FF), up_out.reshape(population, R, FF)))
    weights_rep = jnp.repeat(fitness, R)[:, None]
    gate_scaled = (weights_rep * gate_in.astype(jnp.float32)).astype(jnp.bfloat16)
    up_scaled = (weights_rep * up_in.astype(jnp.float32)).astype(jnp.bfloat16)
    gate_update = (jnp.dot(gate_scaled.T, gate_out, preferred_element_type=jnp.float32) * norm_factor).astype(jnp.bfloat16)
    up_update = (jnp.dot(up_scaled.T, up_out, preferred_element_type=jnp.float32) * norm_factor).astype(jnp.bfloat16)
    return (hidden, gate_update, up_update)
```

```python
import functools
import math

import jax
import jax.numpy as jnp
from jax import lax
from jax.experimental import pallas as pl
from jax.experimental.pallas import tpu as pltpu
from jax.sharding import PartitionSpec as P

R = 4
HASH_MULTIPLIER = 73244475
NOISE_SCALE = math.sqrt(3.0) / 32768.0
PERTURB = 0.3
MINOR = (((1,), (1,)), ((), ()))


def high(value):
    return lax.shift_right_logical(value, jnp.int32(16))


def scramble(value):
    value = (value ^ high(value)) * HASH_MULTIPLIER
    value = (value ^ high(value)) * HASH_MULTIPLIER
    return value ^ high(value)


def mixed(value):
    value = scramble(value)
    return value ^ high(value)


def centered(mix):
    value = mix * HASH_MULTIPLIER
    value = (value ^ high(value)) * HASH_MULTIPLIER
    return ((value ^ high(value)) & 65535).astype(jnp.float32) - 32767.5


def entries(start, rows, length):
    row = lax.broadcasted_iota(jnp.int32, (rows, length), 0)
    column = lax.broadcasted_iota(jnp.int32, (rows, length), 1) + start
    return mixed(column * R + (row & (R - 1)) + 1)


def noise_rows(keys_ref, begin, rows, hashes, length):
    pieces = []
    for t in range(0, rows, 8):
        key = keys_ref[begin + t : begin + t + 8, :]
        pieces.append(
            jnp.concatenate(
                [centered(hashes[:, q : q + 128] ^ key) for q in range(0, length, 128)], axis=1
            )
        )
    return jnp.concatenate(pieces, axis=0)


def base_kernel(x_ref, gate_ref, up_ref, out_ref, gate_buf, up_buf, sems, *, chunk):
    seq = x_ref.shape[0]
    depth = x_ref.shape[1]
    steps = depth // chunk
    copies = []
    for i in range(steps):
        part = pl.ds(i * chunk, chunk)
        pair = (
            pltpu.make_async_copy(gate_ref.at[:, part], gate_buf.at[:, part], sems.at[0, i]),
            pltpu.make_async_copy(up_ref.at[:, part], up_buf.at[:, part], sems.at[1, i]),
        )
        for copy in pair:
            copy.start()
        copies.append(pair)
    gate_sum = up_sum = None
    for i in range(steps):
        part = slice(i * chunk, (i + 1) * chunk)
        x = x_ref[:, part]
        copies[i][0].wait()
        gate = lax.dot_general(x, gate_buf[:, part], MINOR, preferred_element_type=jnp.float32)
        gate_sum = gate if gate_sum is None else gate_sum + gate
        copies[i][1].wait()
        up = lax.dot_general(x, up_buf[:, part], MINOR, preferred_element_type=jnp.float32)
        up_sum = up if up_sum is None else up_sum + up
    out_ref[0:seq] = gate_sum.astype(jnp.bfloat16)
    out_ref[seq : 2 * seq] = up_sum.astype(jnp.bfloat16)


def base_projections(inputs, gate_rows, up_rows):
    seq, depth = inputs.shape
    width = gate_rows.shape[0]
    chunk = 1280
    return pl.pallas_call(
        functools.partial(base_kernel, chunk=chunk),
        out_shape=jax.ShapeDtypeStruct((2 * seq, width), jnp.bfloat16),
        in_specs=[
            pl.BlockSpec(memory_space=pltpu.VMEM),
            pl.BlockSpec(memory_space=pl.ANY),
            pl.BlockSpec(memory_space=pl.ANY),
        ],
        out_specs=pl.BlockSpec(memory_space=pltpu.VMEM),
        scratch_shapes=[
            pltpu.VMEM((width, depth), jnp.bfloat16),
            pltpu.VMEM((width, depth), jnp.bfloat16),
            pltpu.SemaphoreType.DMA((2, depth // chunk)),
        ],
        compiler_params=pltpu.CompilerParams(vmem_limit_bytes=40 * 2**20),
        cost_estimate=pl.CostEstimate(
            flops=4 * seq * depth * width, bytes_accessed=4 * depth * width, transcendentals=0
        ),
        name="base",
    )(inputs, gate_rows, up_rows)


def coeff_kernel(x_ref, keys_ref, out_ref):
    seq, depth = x_ref.shape
    rows = keys_ref.shape[0] // 2
    members = rows // R
    scale = NOISE_SCALE / math.sqrt(depth) * (PERTURB / math.sqrt(R)) * NOISE_SCALE
    hashes = entries(0, 8, depth)
    x = x_ref[...]
    row = lax.broadcasted_iota(jnp.int32, (members * seq, rows + seq), 0)
    lane = lax.broadcasted_iota(jnp.int32, (members * seq, rows + seq), 1)
    own = (row // seq) == (lane // R)
    pick = (lane - rows) == (row % seq)
    for s in range(2):
        noise = noise_rows(keys_ref, s * rows, rows, hashes, depth).astype(jnp.bfloat16)
        padded = jnp.concatenate([noise, jnp.zeros((seq, depth), jnp.bfloat16)], axis=0)
        coeff = lax.dot_general(x, padded, MINOR, preferred_element_type=jnp.float32) * scale
        tiled = jnp.concatenate([coeff] * members, axis=0)
        out_ref[s] = jnp.where(
            lane < rows, jnp.where(own, tiled, 0.0), jnp.where(pick, 1.0, 0.0)
        ).astype(jnp.bfloat16)


def left_operands(inputs, keys):
    seq = inputs.shape[0]
    rows = keys.shape[0] // 2
    return pl.pallas_call(
        coeff_kernel,
        out_shape=jax.ShapeDtypeStruct((2, rows // R * seq, rows + seq), jnp.bfloat16),
        cost_estimate=pl.CostEstimate(flops=10**7, bytes_accessed=10**6, transcendentals=0),
        name="coeff",
    )(inputs, keys)


def hidden_kernel(slot_ref, left_ref, keys_ref, base_ref, other_ref, out_ref, *, group, seq, width):
    g = pl.program_id(0)
    chips = base_ref.shape[0]
    rows = keys_ref.shape[0] // 2
    span = group * width
    hashes = entries(g * span, 8, span)
    pieces = []
    for j in range(group):
        slot = slot_ref[g * group + j]
        index = lax.rem(slot, chips)
        same = base_ref[index]
        sibling = other_ref[index]
        pieces.append(jnp.where(slot < chips, same, sibling))
    base = jnp.concatenate(pieces, axis=1)
    totals = []
    for s in range(2):
        noise = noise_rows(keys_ref, s * rows, rows, hashes, span).astype(jnp.bfloat16)
        right = jnp.concatenate([noise, base[s * seq : (s + 1) * seq]], axis=0)
        totals.append(jnp.dot(left_ref[s], right, preferred_element_type=jnp.float32))
    gate, up = totals
    half = 0.5 * gate
    out_ref[...] = ((half + half * jnp.tanh(half)) * up).astype(jnp.bfloat16)


def hidden_states(slots, left, keys, base, other, seq, width):
    shards = slots.shape[0]
    group = 128 // math.gcd(width, 128)
    total = left.shape[1]
    return pl.pallas_call(
        functools.partial(hidden_kernel, group=group, seq=seq, width=width),
        out_shape=jax.ShapeDtypeStruct((total, shards * width), jnp.bfloat16),
        grid=(shards // group,),
        in_specs=[
            pl.BlockSpec(memory_space=pltpu.SMEM),
            pl.BlockSpec(left.shape, lambda g: (0, 0, 0)),
            pl.BlockSpec(keys.shape, lambda g: (0, 0)),
            pl.BlockSpec(base.shape, lambda g: (0, 0, 0)),
            pl.BlockSpec(other.shape, lambda g: (0, 0, 0)),
        ],
        out_specs=pl.BlockSpec((total, group * width), lambda g: (0, g)),
        cost_estimate=pl.CostEstimate(
            flops=10**8, bytes_accessed=6 * 10**6, transcendentals=2 * 10**6
        ),
        name="hidden",
    )(slots, left, keys, base, other)


def update_kernel(keys_ref, lane_ref, scale_ref, offset_ref, out_ref, cols, rows_buf, *, block, sub):
    step = pl.program_id(0)
    width = out_ref.shape[0]
    terms = keys_ref.shape[0]
    part = width // 9

    @pl.when(step == 0)
    def _():
        def fill(r, carry):
            shape = (part, 128)
            column = lax.broadcasted_iota(jnp.int32, shape, 0) + (offset_ref[0] + r * part)
            lane = lax.broadcasted_iota(jnp.int32, shape, 1)
            hashes = mixed(column * R + (lane & (R - 1)) + 1)
            for t in range(0, terms, 128):
                noise = centered(hashes ^ lane_ref[0:1, t : t + 128])
                cols[pl.ds(pl.multiple_of(r * part, 8), part), t : t + 128] = (
                    noise * scale_ref[0:1, t : t + 128]
                ).astype(jnp.bfloat16)
            return carry

        lax.fori_loop(0, 9, fill, 0)

    def generate(j):
        hashes = entries(step * block + j * sub, 8, sub)
        rows_buf[j % 2] = noise_rows(keys_ref, 0, terms, hashes, sub).astype(jnp.bfloat16)

    count = block // sub
    generate(0)
    for j in range(count):
        if j + 1 < count:
            generate(j + 1)
        out_ref[:, j * sub : (j + 1) * sub] = jnp.dot(
            cols[...], rows_buf[j % 2], preferred_element_type=jnp.float32
        ).astype(jnp.bfloat16)


def update(keys, lane_keys, scales, offset, width, depth, block=1280, sub=256):
    terms = keys.shape[0]
    return pl.pallas_call(
        functools.partial(update_kernel, block=block, sub=sub),
        out_shape=jax.ShapeDtypeStruct((width, depth), jnp.bfloat16),
        grid=(depth // block,),
        in_specs=[
            pl.BlockSpec((terms, 128), lambda i: (0, 0)),
            pl.BlockSpec((1, terms), lambda i: (0, 0)),
            pl.BlockSpec((1, terms), lambda i: (0, 0)),
            pl.BlockSpec(memory_space=pltpu.SMEM),
        ],
        out_specs=pl.BlockSpec((width, block), lambda i: (0, i)),
        scratch_shapes=[
            pltpu.VMEM((width, terms), jnp.bfloat16),
            pltpu.VMEM((2, terms, sub), jnp.bfloat16),
        ],
        cost_estimate=pl.CostEstimate(
            flops=2 * width * terms * depth, bytes_accessed=2 * width * depth, transcendentals=0
        ),
        name="update",
    )(keys, lane_keys, scales, offset)


def ring_order(chips):
    if chips <= 8:
        return list(range(0, chips, 2)) + list(range(chips - 1, 0, -2))
    return list(range(chips))


def lane_keys_of(seeds, stream):
    return jnp.repeat(mixed(seeds * 4 + stream), R)


def per_device(inputs, gate_weight, up_weight, member_seeds, member_ranks):
    devices = lax.axis_size("pop")
    position = lax.axis_index("pop")
    depth, width = gate_weight.shape
    local = member_seeds.shape[0]
    seq = inputs.shape[0]
    population = devices * local
    chips = devices // 2

    known = jnp.stack([member_seeds, member_ranks])[None]
    stride = 1
    while stride < devices:
        pairs = [(i, i ^ stride) for i in range(devices)]
        known = jnp.concatenate([known, lax.ppermute(known, "pop", pairs)], axis=0)
        stride *= 2
    seeds = known[:, 0].reshape(population)
    ranks = known[:, 1].reshape(population)

    base = base_projections(inputs, gate_weight.T, up_weight.T)

    order = ring_order(chips)
    place = [order.index(c) for c in range(chips)]

    def shifted(step):
        return [
            (2 * order[i] + c, 2 * order[(i + step) % chips] + c)
            for i in range(chips)
            for c in range(2)
        ]

    held = {0: base}
    ahead = behind = base
    for k in range(1, chips // 2 + 1):
        ahead = lax.ppermute(ahead, "pop", shifted(1))
        held[k] = ahead
        if k < chips - k:
            behind = lax.ppermute(behind, "pop", shifted(-1))
            held[chips - k] = behind
    mine = jnp.stack([held[d] for d in range(chips)])
    other = lax.ppermute(mine, "pop", [(i, i ^ 1) for i in range(devices)])

    own_out = [
        jnp.broadcast_to(
            jnp.concatenate([lane_keys_of(member_seeds, a), lane_keys_of(member_seeds, b)])[:, None],
            (2 * local * R, 128),
        )
        for a, b in ((0, 2), (1, 3))
    ]
    left = left_operands(inputs, own_out[0])

    fitness = (ranks.astype(jnp.float32) + 0.5) / population - 0.5
    scales = jnp.repeat(fitness, R)[None] * (
        NOISE_SCALE * NOISE_SCALE / math.sqrt(population * R)
    )
    offset = (position * width).astype(jnp.int32).reshape(1)
    updates = []
    for a, b in ((0, 1), (2, 3)):
        keys = jnp.broadcast_to(lane_keys_of(seeds, a)[:, None], (population * R, 128))
        updates.append(update(keys, lane_keys_of(seeds, b)[None], scales, offset, width, depth))

    shard = jnp.arange(devices, dtype=jnp.int32)
    spots = jnp.asarray(place, jnp.int32)
    steps = (spots[position // 2] - spots[shard // 2]) % chips
    slots = steps + ((shard ^ position) & 1) * chips
    hidden = hidden_states(slots, left, own_out[1], mine, other, seq, width)
    return (hidden.reshape(local, seq, -1), updates[0].T, updates[1].T)


def solution(mesh):
    placed = (P("grp", None), P(None, "pop"), P(None, "pop"), P(("grp", "pop")), P(("grp", "pop")))
    return jax.shard_map(
        per_device,
        mesh=mesh,
        in_specs=placed,
        out_specs=(P(("grp", "pop"), None, None), P("grp", "pop"), P("grp", "pop")),
        check_vma=False,
    )
```

```python
import functools
import math

import jax
import jax.numpy as jnp
from jax import lax
from jax.experimental import pallas as pl
from jax.experimental.pallas import tpu as pltpu
from jax.sharding import PartitionSpec as P

R = 4
HASH_MULTIPLIER = 73244475
NOISE_SCALE = math.sqrt(3.0) / 32768.0
PERTURB = 0.3
MINOR = (((1,), (1,)), ((), ()))


def high(value):
    return lax.shift_right_logical(value, jnp.int32(16))


def scramble(value):
    value = (value ^ high(value)) * HASH_MULTIPLIER
    value = (value ^ high(value)) * HASH_MULTIPLIER
    return value ^ high(value)


def mixed(value):
    value = scramble(value)
    return value ^ high(value)


def centered(mix):
    value = mix * HASH_MULTIPLIER
    value = (value ^ high(value)) * HASH_MULTIPLIER
    return ((value ^ high(value)) & 65535).astype(jnp.float32) - 32767.5


def entries(start, rows, length):
    row = lax.broadcasted_iota(jnp.int32, (rows, length), 0)
    column = lax.broadcasted_iota(jnp.int32, (rows, length), 1) + start
    return mixed(column * R + (row & (R - 1)) + 1)


def own_keys(seeds_ref, stream, first):
    row = lax.broadcasted_iota(jnp.int32, (8, 128), 0)
    low = mixed(seeds_ref[first] * 4 + stream)
    top = mixed(seeds_ref[first + 1] * 4 + stream)
    return jnp.where(row < R, low, top)


def own_noise(seeds_ref, stream, hashes, length):
    pieces = []
    for first in range(0, seeds_ref.shape[0], 2):
        key = own_keys(seeds_ref, stream, first)
        pieces.append(
            jnp.concatenate(
                [centered(hashes[:, q : q + 128] ^ key) for q in range(0, length, 128)], axis=1
            )
        )
    return jnp.concatenate(pieces, axis=0).astype(jnp.bfloat16)


SCALARS = pl.BlockSpec(memory_space=pltpu.SMEM)
WHOLE = pl.BlockSpec(memory_space=pltpu.VMEM)


def info_kernel(seeds_ref, ranks_ref, out_ref):
    local = seeds_ref.shape[0]
    row = lax.broadcasted_iota(jnp.int32, out_ref.shape, 0)
    lane = lax.broadcasted_iota(jnp.int32, out_ref.shape, 1) - lax.axis_index("pop") * local
    out = jnp.zeros(out_ref.shape, jnp.int32)
    for m in range(local):
        value = jnp.where(row == 0, seeds_ref[m], jnp.where(row == 1, ranks_ref[m], 0))
        out = jnp.where(lane == m, value, out)
    out_ref[...] = out


def member_info(seeds, ranks, lanes):
    return pl.pallas_call(
        info_kernel,
        out_shape=jax.ShapeDtypeStruct((8, lanes), jnp.int32),
        in_specs=[SCALARS, SCALARS],
        out_specs=WHOLE,
        name="info",
    )(seeds, ranks)


def base_kernel(x_ref, gate_ref, up_ref, out_ref):
    seq, depth = x_ref.shape
    chunk = 1280
    for s, ref in enumerate((gate_ref, up_ref)):
        total = None
        for i in range(0, depth, chunk):
            term = lax.dot_general(
                x_ref[:, i : i + chunk],
                ref[:, i : i + chunk],
                MINOR,
                preferred_element_type=jnp.float32,
            )
            total = term if total is None else total + term
        out_ref[s * seq : (s + 1) * seq] = total.astype(jnp.bfloat16)


def base_projections(inputs, gate_rows, up_rows):
    seq, depth = inputs.shape
    width = gate_rows.shape[0]
    return pl.pallas_call(
        base_kernel,
        out_shape=jax.ShapeDtypeStruct((2 * seq, width), jnp.bfloat16),
        in_specs=[WHOLE, WHOLE, WHOLE],
        out_specs=WHOLE,
        compiler_params=pltpu.CompilerParams(vmem_limit_bytes=4 * 2**20),
        cost_estimate=pl.CostEstimate(
            flops=4 * seq * depth * width, bytes_accessed=4 * depth * width, transcendentals=0
        ),
        name="base",
    )(inputs, gate_rows, up_rows)


def coeff_kernel(seeds_ref, x_ref, out_ref):
    seq, depth = x_ref.shape
    members = seeds_ref.shape[0]
    rows = members * R
    scale = NOISE_SCALE / math.sqrt(depth) * (PERTURB / math.sqrt(R)) * NOISE_SCALE
    hashes = entries(0, 8, depth)
    x = x_ref[...]
    row = lax.broadcasted_iota(jnp.int32, (members * seq, rows + seq), 0)
    lane = lax.broadcasted_iota(jnp.int32, (members * seq, rows + seq), 1)
    own = (row // seq) == (lane // R)
    pick = (lane - rows) == (row % seq)
    for s in range(2):
        noise = own_noise(seeds_ref, 2 * s, hashes, depth)
        padded = jnp.concatenate([noise, jnp.zeros((seq, depth), jnp.bfloat16)], axis=0)
        coeff = lax.dot_general(x, padded, MINOR, preferred_element_type=jnp.float32) * scale
        tiled = jnp.concatenate([coeff] * members, axis=0)
        out_ref[s] = jnp.where(
            lane < rows, jnp.where(own, tiled, 0.0), jnp.where(pick, 1.0, 0.0)
        ).astype(jnp.bfloat16)


def left_operands(seeds, inputs):
    seq = inputs.shape[0]
    members = seeds.shape[0]
    return pl.pallas_call(
        coeff_kernel,
        out_shape=jax.ShapeDtypeStruct((2, members * seq, members * R + seq), jnp.bfloat16),
        in_specs=[SCALARS, WHOLE],
        out_specs=WHOLE,
        cost_estimate=pl.CostEstimate(flops=10**7, bytes_accessed=10**6, transcendentals=0),
        name="coeff",
    )(seeds, inputs)


def ring_place(chip, chips):
    if chips <= 8:
        return jnp.where(chip % 2 == 0, chip // 2, chips - 1 - chip // 2)
    return chip


def hidden_kernel(
    seeds_ref, left_ref, near_ref, near_sib_ref, far_ref, far_sib_ref, out_ref, *, group, seq, width
):
    g = pl.program_id(0)
    reach = near_ref.shape[0] // 2
    chips = near_ref.shape[0] + far_ref.shape[0]
    position = lax.axis_index("pop")
    here = ring_place(position // 2, chips)
    span = group * width
    hashes = entries(g * span, 8, span)
    pieces = []
    for j in range(group):
        shard = g * group + j
        step = lax.rem(here - ring_place(shard // 2, chips) + reach + 2 * chips, chips)
        near = jnp.minimum(step, 2 * reach)
        far = jnp.maximum(step - (2 * reach + 1), 0)
        same = (shard % 2) == (position % 2)
        pieces.append(
            jnp.where(
                step <= 2 * reach,
                jnp.where(same, near_ref[near], near_sib_ref[near]),
                jnp.where(same, far_ref[far], far_sib_ref[far]),
            )
        )
    base = jnp.concatenate(pieces, axis=1)
    totals = []
    for s in range(2):
        noise = own_noise(seeds_ref, 2 * s + 1, hashes, span)
        right = jnp.concatenate([noise, base[s * seq : (s + 1) * seq]], axis=0)
        totals.append(jnp.dot(left_ref[s], right, preferred_element_type=jnp.float32))
    gate, up = totals
    half = 0.5 * gate
    out_ref[...] = ((half + half * jnp.tanh(half)) * up).astype(jnp.bfloat16)


def hidden_states(seeds, left, shards, width, seq):
    total = left.shape[1]
    count = 2 * (shards[0].shape[0] + shards[2].shape[0])
    group = 128 // math.gcd(width, 128)
    return pl.pallas_call(
        functools.partial(hidden_kernel, group=group, seq=seq, width=width),
        out_shape=jax.ShapeDtypeStruct((total, count * width), jnp.bfloat16),
        grid=(count // group,),
        in_specs=[SCALARS] + [WHOLE] * 5,
        out_specs=pl.BlockSpec((total, group * width), lambda g: (0, g)),
        cost_estimate=pl.CostEstimate(
            flops=10**8, bytes_accessed=6 * 10**6, transcendentals=2 * 10**6
        ),
        name="hidden",
    )(seeds, left, *shards)


def columns_kernel(info_ref, cols_ref, keys_ref, *, population):
    width, terms = cols_ref.shape[1:]
    norm = NOISE_SCALE * NOISE_SCALE / math.sqrt(population * R)
    seeds = info_ref[0:1, 0:population]
    ranks = info_ref[1:2, 0:population]
    scale = ((ranks.astype(jnp.float32) + 0.5) / population - 0.5) * norm
    scales = jnp.concatenate([scale] * R, axis=1)
    wide = jnp.concatenate([seeds] * R, axis=1)
    for s in range(2):
        for t in range(0, population, 64):
            square = jnp.broadcast_to(seeds[:, t : t + 64].astype(jnp.float32), (128, 64))
            keys_ref[s, t : t + 64, :] = mixed(square.T.astype(jnp.int32) * 4 + 2 * s)
    lane_keys = [mixed(wide * 4 + (2 * s + 1)) for s in range(2)]
    part = width // 9
    offset = lax.axis_index("pop") * width

    def fill(r, carry):
        column = lax.broadcasted_iota(jnp.int32, (part, 128), 0) + (offset + r * part)
        lane = lax.broadcasted_iota(jnp.int32, (part, 128), 1)
        where = pl.ds(pl.multiple_of(r * part, 8), part)
        for t in range(0, terms, 128):
            hashes = mixed(column * R + (lane + t) // population + 1)
            for s in range(2):
                noise = centered(hashes ^ lane_keys[s][:, t : t + 128])
                cols_ref[s, where, t : t + 128] = (noise * scales[:, t : t + 128]).astype(jnp.bfloat16)
        return carry

    lax.fori_loop(0, 9, fill, 0)


def update_columns(info, population, width):
    return pl.pallas_call(
        functools.partial(columns_kernel, population=population),
        out_shape=(
            jax.ShapeDtypeStruct((2, width, population * R), jnp.bfloat16),
            jax.ShapeDtypeStruct((2, population, 128), jnp.int32),
        ),
        in_specs=[WHOLE],
        out_specs=(WHOLE, WHOLE),
        cost_estimate=pl.CostEstimate(flops=10**7, bytes_accessed=10**6, transcendentals=0),
        name="columns",
    )(info)


def update_kernel(keys_ref, cols_ref, *rest, start, block, sub):
    out_ref, rows_buf = rest[-2:]
    step = pl.program_id(0) + start
    population = keys_ref.shape[1]

    def generate(j):
        hashes = entries(step * block + j * sub, 8, sub)
        slot = j % 2
        for k in range(R):
            for q in range(0, sub, 128):
                entry = jnp.broadcast_to(hashes[k : k + 1, q : q + 128], (16, 128))
                for t in range(0, population, 16):
                    at = k * population + t
                    rows_buf[slot, at : at + 16, q : q + 128] = centered(
                        entry ^ keys_ref[0, t : t + 16, :]
                    ).astype(jnp.bfloat16)

    count = block // sub
    generate(0)
    for j in range(count):
        if j + 1 < count:
            generate(j + 1)
        out_ref[:, j * sub : (j + 1) * sub] = jnp.dot(
            cols_ref[0], rows_buf[j % 2], preferred_element_type=jnp.float32
        ).astype(jnp.bfloat16)


def update(keys, cols, stream, depth, piece, pieces, onto=None, block=1280, sub=256):
    width, terms = cols.shape[1:]
    population = keys.shape[1]
    steps = depth // block // pieces
    start = piece * steps
    operands = (keys, cols) + (() if onto is None else (onto,))
    return pl.pallas_call(
        functools.partial(update_kernel, start=start, block=block, sub=sub),
        out_shape=jax.ShapeDtypeStruct((width, depth), jnp.bfloat16),
        grid=(steps,),
        in_specs=[
            pl.BlockSpec((1, population, 128), lambda i: (stream, 0, 0)),
            pl.BlockSpec((1, width, terms), lambda i: (stream, 0, 0)),
        ]
        + ([] if onto is None else [pl.BlockSpec(memory_space=pl.ANY)]),
        out_specs=pl.BlockSpec((width, block), lambda i: (0, i + start)),
        scratch_shapes=[pltpu.VMEM((2, terms, sub), jnp.bfloat16)],
        input_output_aliases={} if onto is None else {2: 0},
        cost_estimate=pl.CostEstimate(
            flops=2 * width * terms * depth // pieces,
            bytes_accessed=2 * width * depth // pieces,
            transcendentals=0,
        ),
        name="update",
    )(*operands)


def ring_order(chips):
    if chips <= 8:
        return list(range(0, chips, 2)) + list(range(chips - 1, 0, -2))
    return list(range(chips))


def after(value, *others):
    return lax.optimization_barrier((value, *others))[0]


def per_device(inputs, gate_weight, up_weight, member_seeds, member_ranks):
    devices = lax.axis_size("pop")
    depth, width = gate_weight.shape
    local = member_seeds.shape[0]
    seq = inputs.shape[0]
    population = devices * local
    chips = devices // 2

    info = member_info(member_seeds, member_ranks, -(-population // 128) * 128)
    known = [info]
    stride = 1
    while stride < devices:
        pairs = [(i, i ^ stride) for i in range(devices)]
        info = info + lax.ppermute(info, "pop", pairs)
        known.append(info)
        stride *= 2

    left = left_operands(member_seeds, inputs)
    base = base_projections(after(inputs, known[-2]), gate_weight.T, up_weight.T)
    cols, keys = update_columns(info, population, width)

    order = ring_order(chips)

    def shifted(step):
        return [
            (2 * order[i] + c, 2 * order[(i + step) % chips] + c)
            for i in range(chips)
            for c in range(2)
        ]

    siblings = [(i, i ^ 1) for i in range(devices)]
    reach = chips // 4
    held = {0: base}
    ahead = behind = base
    updates = [None, None]
    work = [(s, piece) for s in range(2) for piece in range(2)]
    done = 0
    for k in range(1, chips // 2 + 1):
        ahead = lax.ppermute(ahead, "pop", shifted(1))
        held[k] = ahead
        if k < chips - k:
            behind = lax.ppermute(behind, "pop", shifted(-1))
            held[chips - k] = behind
        if k == reach:
            near = jnp.stack([held[(d - reach) % chips] for d in range(2 * reach + 1)])
            near_sib = lax.ppermute(near, "pop", siblings)
        due = (len(work) * k) // (chips // 2 + 1)
        for s, piece in work[done:due]:
            updates[s] = update(keys, cols, s, depth, piece, 2, updates[s])
            ahead, behind = after(ahead, updates[s]), after(behind, updates[s])
        done = due
    far = jnp.stack([held[d] for d in range(reach + 1, chips - reach)])
    far_sib = lax.ppermute(far, "pop", siblings)
    for s, piece in work[done:]:
        updates[s] = update(keys, cols, s, depth, piece, 2, updates[s])
    hidden = hidden_states(
        after(member_seeds, *updates), left, (near, near_sib, far, far_sib), width, seq
    )
    return (hidden.reshape(local, seq, -1), updates[0].T, updates[1].T)


def solution(mesh):
    placed = (P("grp", None), P(None, "pop"), P(None, "pop"), P(("grp", "pop")), P(("grp", "pop")))
    return jax.shard_map(
        per_device,
        mesh=mesh,
        in_specs=placed,
        out_specs=(P(("grp", "pop"), None, None), P("grp", "pop"), P("grp", "pop")),
        check_vma=False,
    )
```

```python
import functools
import math

import jax
import jax.numpy as jnp
from jax import lax
from jax.experimental import pallas as pl
from jax.experimental.pallas import tpu as pltpu
from jax.sharding import PartitionSpec as P

R = 4
HASH_MULTIPLIER = 73244475
NOISE_SCALE = math.sqrt(3.0) / 32768.0
PERTURB = 0.3
MINOR = (((1,), (1,)), ((), ()))


def high(value):
    return lax.shift_right_logical(value, jnp.int32(16))


def scramble(value):
    value = (value ^ high(value)) * HASH_MULTIPLIER
    value = (value ^ high(value)) * HASH_MULTIPLIER
    return value ^ high(value)


def mixed(value):
    value = scramble(value)
    return value ^ high(value)


def centered(mix):
    value = mix * HASH_MULTIPLIER
    value = (value ^ high(value)) * HASH_MULTIPLIER
    return ((value ^ high(value)) & 65535).astype(jnp.float32) - 32767.5


def entries(start, rows, length):
    row = lax.broadcasted_iota(jnp.int32, (rows, length), 0)
    column = lax.broadcasted_iota(jnp.int32, (rows, length), 1) + start
    return mixed(column * R + (row & (R - 1)) + 1)


def own_keys(seeds_ref, stream, first):
    row = lax.broadcasted_iota(jnp.int32, (8, 128), 0)
    low = mixed(seeds_ref[first] * 4 + stream)
    top = mixed(seeds_ref[first + 1] * 4 + stream)
    return jnp.where(row < R, low, top)


def own_noise(seeds_ref, stream, hashes, length):
    pieces = []
    for first in range(0, seeds_ref.shape[0], 2):
        key = own_keys(seeds_ref, stream, first)
        pieces.append(
            jnp.concatenate(
                [centered(hashes[:, q : q + 128] ^ key) for q in range(0, length, 128)], axis=1
            )
        )
    return jnp.concatenate(pieces, axis=0).astype(jnp.bfloat16)


SCALARS = pl.BlockSpec(memory_space=pltpu.SMEM)
WHOLE = pl.BlockSpec(memory_space=pltpu.VMEM)
PLACED = pl.BlockSpec(memory_space=pl.ANY)


def room(mebibytes):
    return pltpu.CompilerParams(vmem_limit_bytes=mebibytes * 2**20)


def info_kernel(seeds_ref, ranks_ref, out_ref):
    local = seeds_ref.shape[0]
    row = lax.broadcasted_iota(jnp.int32, out_ref.shape, 0)
    lane = lax.broadcasted_iota(jnp.int32, out_ref.shape, 1) - lax.axis_index("pop") * local
    out = jnp.zeros(out_ref.shape, jnp.int32)
    for m in range(local):
        value = jnp.where(row == 0, seeds_ref[m], jnp.where(row == 1, ranks_ref[m], 0))
        out = jnp.where(lane == m, value, out)
    out_ref[...] = out


def member_info(seeds, ranks, lanes):
    return pl.pallas_call(
        info_kernel,
        out_shape=jax.ShapeDtypeStruct((8, lanes), jnp.int32),
        in_specs=[SCALARS, SCALARS],
        out_specs=WHOLE,
        compiler_params=room(2),
        name="info",
    )(seeds, ranks)


def base_kernel(x_ref, gate_ref, up_ref, out_ref, gate_buf, up_buf, sems, *, chunk):
    seq = x_ref.shape[0]
    depth = x_ref.shape[1]
    steps = depth // chunk
    copies = []
    for i in range(steps):
        part = pl.ds(i * chunk, chunk)
        pair = (
            pltpu.make_async_copy(gate_ref.at[:, part], gate_buf.at[:, part], sems.at[0, i]),
            pltpu.make_async_copy(up_ref.at[:, part], up_buf.at[:, part], sems.at[1, i]),
        )
        for copy in pair:
            copy.start()
        copies.append(pair)
    gate_sum = up_sum = None
    for i in range(steps):
        part = slice(i * chunk, (i + 1) * chunk)
        x = x_ref[:, part]
        copies[i][0].wait()
        gate = lax.dot_general(x, gate_buf[:, part], MINOR, preferred_element_type=jnp.float32)
        gate_sum = gate if gate_sum is None else gate_sum + gate
        copies[i][1].wait()
        up = lax.dot_general(x, up_buf[:, part], MINOR, preferred_element_type=jnp.float32)
        up_sum = up if up_sum is None else up_sum + up
    out_ref[0:seq] = gate_sum.astype(jnp.bfloat16)
    out_ref[seq : 2 * seq] = up_sum.astype(jnp.bfloat16)


def base_projections(inputs, gate_rows, up_rows):
    seq, depth = inputs.shape
    width = gate_rows.shape[0]
    chunk = 1280
    return pl.pallas_call(
        functools.partial(base_kernel, chunk=chunk),
        out_shape=jax.ShapeDtypeStruct((2 * seq, width), jnp.bfloat16),
        in_specs=[
            WHOLE,
            PLACED,
            PLACED,
        ],
        out_specs=WHOLE,
        scratch_shapes=[
            pltpu.VMEM((width, depth), jnp.bfloat16),
            pltpu.VMEM((width, depth), jnp.bfloat16),
            pltpu.SemaphoreType.DMA((2, depth // chunk)),
        ],
        compiler_params=room(62),
        cost_estimate=pl.CostEstimate(
            flops=4 * seq * depth * width, bytes_accessed=4 * depth * width, transcendentals=0
        ),
        name="base",
    )(inputs, gate_rows, up_rows)


def coeff_kernel(seeds_ref, x_ref, out_ref):
    seq, depth = x_ref.shape
    members = seeds_ref.shape[0]
    rows = members * R
    scale = NOISE_SCALE / math.sqrt(depth) * (PERTURB / math.sqrt(R)) * NOISE_SCALE
    hashes = entries(0, 8, depth)
    x = x_ref[...]
    row = lax.broadcasted_iota(jnp.int32, (members * seq, rows + seq), 0)
    lane = lax.broadcasted_iota(jnp.int32, (members * seq, rows + seq), 1)
    own = (row // seq) == (lane // R)
    pick = (lane - rows) == (row % seq)
    for s in range(2):
        noise = own_noise(seeds_ref, 2 * s, hashes, depth)
        padded = jnp.concatenate([noise, jnp.zeros((seq, depth), jnp.bfloat16)], axis=0)
        coeff = lax.dot_general(x, padded, MINOR, preferred_element_type=jnp.float32) * scale
        tiled = jnp.concatenate([coeff] * members, axis=0)
        out_ref[s] = jnp.where(
            lane < rows, jnp.where(own, tiled, 0.0), jnp.where(pick, 1.0, 0.0)
        ).astype(jnp.bfloat16)


def left_operands(seeds, inputs):
    seq = inputs.shape[0]
    members = seeds.shape[0]
    return pl.pallas_call(
        coeff_kernel,
        out_shape=jax.ShapeDtypeStruct((2, members * seq, members * R + seq), jnp.bfloat16),
        in_specs=[SCALARS, WHOLE],
        out_specs=WHOLE,
        compiler_params=room(12),
        cost_estimate=pl.CostEstimate(flops=10**7, bytes_accessed=10**6, transcendentals=0),
        name="coeff",
    )(seeds, inputs)


def noise_kernel(seeds_ref, out_ref, *, part):
    for start in range(0, out_ref.shape[2], part):
        hashes = entries(start, 8, part)
        for s in range(2):
            out_ref[s, :, start : start + part] = own_noise(seeds_ref, 2 * s + 1, hashes, part)


def output_noise(seeds, total):
    return pl.pallas_call(
        functools.partial(noise_kernel, part=1536),
        out_shape=jax.ShapeDtypeStruct((2, seeds.shape[0] * R, total), jnp.bfloat16),
        in_specs=[SCALARS],
        out_specs=WHOLE,
        compiler_params=room(8),
        cost_estimate=pl.CostEstimate(flops=10**7, bytes_accessed=10**6, transcendentals=0),
        name="noise",
    )(seeds)


def ring_place(chip, chips):
    if chips <= 8:
        return jnp.where(chip % 2 == 0, chip // 2, chips - 1 - chip // 2)
    return chip


def hidden_kernel(
    left_ref,
    noise_ref,
    near_ref,
    near_sib_ref,
    far_ref,
    far_sib_ref,
    out_ref,
    base,
    buf,
    sems,
    *,
    seq,
    sub,
    chunk,
):
    width = near_ref.shape[2]
    reach = near_ref.shape[0] // 2
    chips = near_ref.shape[0] + far_ref.shape[0]
    group = 128 // math.gcd(width, 128)
    position = lax.axis_index("pop")
    here = ring_place(position // 2, chips)
    for first in range(0, 2 * chips, group):
        pieces = []
        for shard in range(first, first + group):
            step = lax.rem(here - ring_place(shard // 2, chips) + reach + 2 * chips, chips)
            near = jnp.minimum(step, 2 * reach)
            far = jnp.maximum(step - (2 * reach + 1), 0)
            same = (position % 2) == (shard % 2)
            pieces.append(
                jnp.where(
                    step <= 2 * reach,
                    jnp.where(same, near_ref[near], near_sib_ref[near]),
                    jnp.where(same, far_ref[far], far_sib_ref[far]),
                )
            )
        base[:, first * width : (first + group) * width] = jnp.concatenate(pieces, axis=1)
    copies = []
    for begin in range(0, out_ref.shape[1], sub):
        part = slice(begin, begin + sub)
        totals = []
        for s in range(2):
            right = jnp.concatenate(
                [noise_ref[s, :, part], base[s * seq : (s + 1) * seq, part]], axis=0
            )
            totals.append(jnp.dot(left_ref[s], right, preferred_element_type=jnp.float32))
        half = 0.5 * totals[0]
        buf[:, part] = ((half + half * jnp.tanh(half)) * totals[1]).astype(jnp.bfloat16)
        if (begin + sub) % chunk == 0:
            i = begin // chunk
            span = pl.ds(i * chunk, chunk)
            copies.append(
                pltpu.make_async_copy(buf.at[:, span], out_ref.at[:, span], sems.at[i])
            )
            copies[-1].start()
    for copy in copies:
        copy.wait()


def hidden_states(left, noise, shards, width, seq, sub=256, chunk=1536):
    rows = left.shape[1]
    total = noise.shape[2]
    return pl.pallas_call(
        functools.partial(hidden_kernel, seq=seq, sub=sub, chunk=chunk),
        out_shape=jax.ShapeDtypeStruct((rows, total), jnp.bfloat16),
        in_specs=[WHOLE] * 6,
        out_specs=PLACED,
        scratch_shapes=[
            pltpu.VMEM((2 * seq, total), jnp.bfloat16),
            pltpu.VMEM((rows, total), jnp.bfloat16),
            pltpu.SemaphoreType.DMA((total // chunk,)),
        ],
        compiler_params=room(16),
        cost_estimate=pl.CostEstimate(
            flops=10**8, bytes_accessed=6 * 10**6, transcendentals=2 * 10**6
        ),
        name="hidden",
    )(left, noise, *shards)


def columns_kernel(info_ref, got_ref, cols_ref, keys_ref, *, population):
    width, terms = cols_ref.shape[1:]
    norm = NOISE_SCALE * NOISE_SCALE / math.sqrt(population * R)
    info = info_ref[...] + got_ref[...]
    seeds = info[0:1, 0:population]
    ranks = info[1:2, 0:population]
    scale = ((ranks.astype(jnp.float32) + 0.5) / population - 0.5) * norm
    scales = jnp.concatenate([scale] * R, axis=1)
    wide = jnp.concatenate([seeds] * R, axis=1)
    for s in range(2):
        for t in range(0, population, 64):
            square = jnp.broadcast_to(seeds[:, t : t + 64].astype(jnp.float32), (128, 64))
            keys_ref[s, t : t + 64, :] = mixed(square.T.astype(jnp.int32) * 4 + 2 * s)
    lane_keys = [mixed(wide * 4 + (2 * s + 1)) for s in range(2)]
    part = width // 9
    offset = lax.axis_index("pop") * width

    def fill(r, carry):
        column = lax.broadcasted_iota(jnp.int32, (part, 128), 0) + (offset + r * part)
        lane = lax.broadcasted_iota(jnp.int32, (part, 128), 1)
        where = pl.ds(pl.multiple_of(r * part, 8), part)
        for t in range(0, terms, 128):
            hashes = mixed(column * R + (lane + t) // population + 1)
            for s in range(2):
                noise = centered(hashes ^ lane_keys[s][:, t : t + 128])
                cols_ref[s, where, t : t + 128] = (noise * scales[:, t : t + 128]).astype(jnp.bfloat16)
        return carry

    lax.fori_loop(0, 9, fill, 0)


def update_columns(info, got, population, width):
    return pl.pallas_call(
        functools.partial(columns_kernel, population=population),
        out_shape=(
            jax.ShapeDtypeStruct((2, width, population * R), jnp.bfloat16),
            jax.ShapeDtypeStruct((2, population, 128), jnp.int32),
        ),
        in_specs=[WHOLE, WHOLE],
        out_specs=(WHOLE, WHOLE),
        compiler_params=room(8),
        cost_estimate=pl.CostEstimate(flops=10**7, bytes_accessed=10**6, transcendentals=0),
        name="columns",
    )(info, got)


def update_kernel(keys_ref, cols_ref, out_ref, buf, rows_buf, sems, *, stream, sub, chunk):
    depth = out_ref.shape[1]
    population = keys_ref.shape[1]

    def generate(j):
        hashes = entries(j * sub, 8, sub)
        slot = j % 2
        for k in range(R):
            for q in range(0, sub, 128):
                entry = jnp.broadcast_to(hashes[k : k + 1, q : q + 128], (16, 128))
                for t in range(0, population, 16):
                    at = k * population + t
                    rows_buf[slot, at : at + 16, q : q + 128] = centered(
                        entry ^ keys_ref[stream, t : t + 16, :]
                    ).astype(jnp.bfloat16)

    count = depth // sub
    copies = []
    generate(0)
    for j in range(count):
        if j + 1 < count:
            generate(j + 1)
        buf[:, j * sub : (j + 1) * sub] = jnp.dot(
            cols_ref[stream], rows_buf[j % 2], preferred_element_type=jnp.float32
        ).astype(jnp.bfloat16)
        if (j + 1) * sub % chunk == 0:
            i = j * sub // chunk
            span = pl.ds(i * chunk, chunk)
            copies.append(
                pltpu.make_async_copy(buf.at[:, span], out_ref.at[:, span], sems.at[i])
            )
            copies[-1].start()
    for copy in copies:
        copy.wait()


def update(keys, cols, stream, depth, sub=256, chunk=512):
    width, terms = cols.shape[1:]
    return pl.pallas_call(
        functools.partial(update_kernel, stream=stream, sub=sub, chunk=chunk),
        out_shape=jax.ShapeDtypeStruct((width, depth), jnp.bfloat16),
        in_specs=[WHOLE, WHOLE],
        out_specs=PLACED,
        scratch_shapes=[
            pltpu.VMEM((width, depth), jnp.bfloat16),
            pltpu.VMEM((2, terms, sub), jnp.bfloat16),
            pltpu.SemaphoreType.DMA((depth // chunk,)),
        ],
        compiler_params=room(24),
        cost_estimate=pl.CostEstimate(
            flops=2 * width * terms * depth, bytes_accessed=2 * width * depth, transcendentals=0
        ),
        name="update",
    )(keys, cols)


def ring_order(chips):
    if chips <= 8:
        return list(range(0, chips, 2)) + list(range(chips - 1, 0, -2))
    return list(range(chips))


def together(*values):
    return lax.optimization_barrier(values)


def per_device(inputs, gate_weight, up_weight, member_seeds, member_ranks):
    devices = lax.axis_size("pop")
    depth, width = gate_weight.shape
    local = member_seeds.shape[0]
    seq = inputs.shape[0]
    population = devices * local
    chips = devices // 2
    reach = chips // 4
    order = ring_order(chips)
    siblings = [(i, i ^ 1) for i in range(devices)]

    def shifted(step):
        return [
            (2 * order[i] + c, 2 * order[(i + step) % chips] + c)
            for i in range(chips)
            for c in range(2)
        ]

    info = member_info(member_seeds, member_ranks, -(-population // 128) * 128)
    got = lax.ppermute(info, "pop", siblings)
    base = base_projections(inputs, gate_weight.T, up_weight.T)
    info = info + got

    held = {0: base}
    ahead = behind = base
    stride = 2
    left = noise = cols = keys = near_sib = None
    updates = []
    for k in range(1, chips // 2 + 1):
        if stride < devices:
            info, ahead, behind = together(info, ahead, behind)
            got = lax.ppermute(info, "pop", [(i, i ^ stride) for i in range(devices)])
            stride *= 2
            last = stride == devices
        else:
            last = False
        ahead = lax.ppermute(ahead, "pop", shifted(1))
        held[k] = ahead
        if k < chips - k:
            behind = lax.ppermute(behind, "pop", shifted(-1))
            held[chips - k] = behind
        if k == 1:
            left = left_operands(member_seeds, together(inputs, base)[0])
            ahead, behind, left = together(ahead, behind, left)
        elif k == 2:
            noise = output_noise(together(member_seeds, info)[0], devices * width)
            ahead, behind, noise = together(ahead, behind, noise)
        if k == reach:
            near = jnp.stack([held[(d - reach) % chips] for d in range(2 * reach + 1)])
            near_sib = lax.ppermute(near, "pop", siblings)
        if last:
            cols, keys = update_columns(info, got, population, width)
            ahead, behind, cols = together(ahead, behind, cols)
        elif cols is None:
            info = info + got
    far = jnp.stack([held[d] for d in range(reach + 1, chips - reach)])
    first = update(keys, cols, 0, depth)
    far, first, cols = together(far, first, cols)
    far_sib = lax.ppermute(far, "pop", siblings)
    second = update(keys, cols, 1, depth)
    noise = together(noise, second)[0]
    hidden = hidden_states(left, noise, (near, near_sib, far, far_sib), width, seq)
    return (hidden.reshape(local, seq, -1), first.T, second.T)


def solution(mesh):
    placed = (P("grp", None), P(None, "pop"), P(None, "pop"), P(("grp", "pop")), P(("grp", "pop")))
    return jax.shard_map(
        per_device,
        mesh=mesh,
        in_specs=placed,
        out_specs=(P(("grp", "pop"), None, None), P("grp", "pop"), P("grp", "pop")),
        check_vma=False,
    )
```

```python
import functools
import math

import jax
import jax.numpy as jnp
from jax import lax
from jax.experimental import pallas as pl
from jax.experimental.pallas import tpu as pltpu
from jax.sharding import PartitionSpec as P

R = 4
HASH_MULTIPLIER = 73244475
NOISE_SCALE = math.sqrt(3.0) / 32768.0
PERTURB = 0.3
MINOR = (((1,), (1,)), ((), ()))


def high(value):
    return lax.shift_right_logical(value, jnp.int32(16))


def scramble(value):
    value = (value ^ high(value)) * HASH_MULTIPLIER
    value = (value ^ high(value)) * HASH_MULTIPLIER
    return value ^ high(value)


def mixed(value):
    value = scramble(value)
    return value ^ high(value)


def centered(mix):
    value = mix * HASH_MULTIPLIER
    value = (value ^ high(value)) * HASH_MULTIPLIER
    return ((value ^ high(value)) & 65535).astype(jnp.float32) - 32767.5


def entries(start, rows, length):
    row = lax.broadcasted_iota(jnp.int32, (rows, length), 0)
    column = lax.broadcasted_iota(jnp.int32, (rows, length), 1) + start
    return mixed(column * R + (row & (R - 1)) + 1)


def own_keys(seeds_ref, stream, first):
    row = lax.broadcasted_iota(jnp.int32, (8, 128), 0)
    low = mixed(seeds_ref[first] * 4 + stream)
    top = mixed(seeds_ref[first + 1] * 4 + stream)
    return jnp.where(row < R, low, top)


def own_noise(seeds_ref, stream, hashes, length):
    pieces = []
    for first in range(0, seeds_ref.shape[0], 2):
        key = own_keys(seeds_ref, stream, first)
        pieces.append(
            jnp.concatenate(
                [centered(hashes[:, q : q + 128] ^ key) for q in range(0, length, 128)], axis=1
            )
        )
    return jnp.concatenate(pieces, axis=0).astype(jnp.bfloat16)


SCALARS = pl.BlockSpec(memory_space=pltpu.SMEM)
WHOLE = pl.BlockSpec(memory_space=pltpu.VMEM)
PLACED = pl.BlockSpec(memory_space=pl.ANY)


def room(mebibytes):
    return pltpu.CompilerParams(vmem_limit_bytes=mebibytes * 2**20)


def base_kernel(
    seeds_ref, ranks_ref, x_ref, gate_ref, up_ref, out_ref, info_ref, own, x_buf, gate_buf, up_buf, small, sems, *, pieces, ahead
):
    seq = x_buf.shape[0]
    first = [
        pltpu.make_async_copy(x_ref, x_buf, small.at[0]),
        pltpu.make_async_copy(seeds_ref, own.at[0], small.at[1]),
        pltpu.make_async_copy(ranks_ref, own.at[1], small.at[2]),
    ]
    copies = []
    begin = 0
    for i, size in enumerate(pieces):
        part = pl.ds(begin, size)
        copies.append(
            (
                pltpu.make_async_copy(gate_ref.at[:, part], gate_buf.at[:, part], sems.at[0, i]),
                pltpu.make_async_copy(up_ref.at[:, part], up_buf.at[:, part], sems.at[1, i]),
            )
        )
        begin += size
    for copy in first:
        copy.start()
    for pair in copies[:ahead]:
        for copy in pair:
            copy.start()
    for copy in first:
        copy.wait()
    local = own.shape[1]
    row = lax.broadcasted_iota(jnp.int32, info_ref.shape, 0)
    lane = lax.broadcasted_iota(jnp.int32, info_ref.shape, 1) - lax.axis_index("pop") * local
    info = jnp.zeros(info_ref.shape, jnp.int32)
    for m in range(local):
        value = jnp.where(row == 0, own[0, m], jnp.where(row == 1, own[1, m], 0))
        info = jnp.where(lane == m, value, info)
    info_ref[...] = info
    sums = [None, None]
    begin = 0
    for i, size in enumerate(pieces):
        for copy in copies[i]:
            copy.wait()
        if i + ahead < len(pieces):
            for copy in copies[i + ahead]:
                copy.start()
        part = slice(begin, begin + size)
        for s, buf in enumerate((gate_buf, up_buf)):
            term = lax.dot_general(
                x_buf[:, part], buf[:, part], MINOR, preferred_element_type=jnp.float32
            )
            sums[s] = term if sums[s] is None else sums[s] + term
        begin += size
    for s in range(2):
        out_ref[s * seq : (s + 1) * seq] = sums[s].astype(jnp.bfloat16)


def base_projections(seeds, ranks, inputs, gate_rows, up_rows, lanes):
    seq, depth = inputs.shape
    width = gate_rows.shape[0]
    pieces = (512,) + (1024,) * (depth // 1024 - 1) + (512,)
    return pl.pallas_call(
        functools.partial(base_kernel, pieces=pieces, ahead=3),
        out_shape=(
            jax.ShapeDtypeStruct((2 * seq, width), jnp.bfloat16),
            jax.ShapeDtypeStruct((8, lanes), jnp.int32),
        ),
        in_specs=[PLACED] * 5,
        out_specs=(WHOLE, WHOLE),
        scratch_shapes=[
            pltpu.SMEM((2, seeds.shape[0]), jnp.int32),
            pltpu.VMEM((seq, depth), jnp.bfloat16),
            pltpu.VMEM((width, depth), jnp.bfloat16),
            pltpu.VMEM((width, depth), jnp.bfloat16),
            pltpu.SemaphoreType.DMA((3,)),
            pltpu.SemaphoreType.DMA((2, len(pieces))),
        ],
        compiler_params=room(57),
        cost_estimate=pl.CostEstimate(
            flops=4 * seq * depth * width, bytes_accessed=4 * depth * width, transcendentals=0
        ),
        name="base",
    )(seeds, ranks, inputs, gate_rows, up_rows)


def coeff_kernel(seeds_ref, x_ref, out_ref):
    seq, depth = x_ref.shape
    members = seeds_ref.shape[0]
    rows = members * R
    scale = NOISE_SCALE / math.sqrt(depth) * (PERTURB / math.sqrt(R)) * NOISE_SCALE
    hashes = entries(0, 8, depth)
    x = x_ref[...]
    row = lax.broadcasted_iota(jnp.int32, (members * seq, rows + seq), 0)
    lane = lax.broadcasted_iota(jnp.int32, (members * seq, rows + seq), 1)
    own = (row // seq) == (lane // R)
    pick = (lane - rows) == (row % seq)
    for s in range(2):
        noise = own_noise(seeds_ref, 2 * s, hashes, depth)
        padded = jnp.concatenate([noise, jnp.zeros((seq, depth), jnp.bfloat16)], axis=0)
        coeff = lax.dot_general(x, padded, MINOR, preferred_element_type=jnp.float32) * scale
        tiled = jnp.concatenate([coeff] * members, axis=0)
        out_ref[s] = jnp.where(
            lane < rows, jnp.where(own, tiled, 0.0), jnp.where(pick, 1.0, 0.0)
        ).astype(jnp.bfloat16)


def left_operands(seeds, inputs):
    seq = inputs.shape[0]
    members = seeds.shape[0]
    return pl.pallas_call(
        coeff_kernel,
        out_shape=jax.ShapeDtypeStruct((2, members * seq, members * R + seq), jnp.bfloat16),
        in_specs=[SCALARS, WHOLE],
        out_specs=WHOLE,
        compiler_params=room(12),
        cost_estimate=pl.CostEstimate(flops=10**7, bytes_accessed=10**6, transcendentals=0),
        name="coeff",
    )(seeds, inputs)


def noise_kernel(seeds_ref, out_ref, *, part):
    for start in range(0, out_ref.shape[2], part):
        hashes = entries(start, 8, part)
        for s in range(2):
            out_ref[s, :, start : start + part] = own_noise(seeds_ref, 2 * s + 1, hashes, part)


def output_noise(seeds, total):
    return pl.pallas_call(
        functools.partial(noise_kernel, part=1536),
        out_shape=jax.ShapeDtypeStruct((2, seeds.shape[0] * R, total), jnp.bfloat16),
        in_specs=[SCALARS],
        out_specs=WHOLE,
        compiler_params=room(8),
        cost_estimate=pl.CostEstimate(flops=10**7, bytes_accessed=10**6, transcendentals=0),
        name="noise",
    )(seeds)


def chip_at(place, chips):
    if chips <= 8:
        return jnp.where(place < chips // 2, 2 * place, 2 * (chips - 1 - place) + 1)
    return place


def ring_place(chip, chips):
    if chips <= 8:
        return jnp.where(chip % 2 == 0, chip // 2, chips - 1 - chip // 2)
    return chip


def hidden_kernel(left_ref, noise_ref, *rest, seq, sub, chunk):
    shard_refs, (out_ref, ordered, base, buf, sems) = rest[:-5], rest[-5:]
    chips = len(shard_refs)
    reach = chips // 2
    width = base.shape[1] // (2 * chips)
    group = 128 // math.gcd(width, 128)
    position = lax.axis_index("pop")
    core = lax.rem(position, 2)
    here = ring_place(position // 2, chips)
    for i, ref in enumerate(shard_refs):
        step = i if i <= reach else i - reach
        toward = 2 * core - 1 if i <= reach else 1 - 2 * core
        chip = chip_at(lax.rem(here + toward * step + chips, chips), chips)
        owner = core if i <= reach else 1 - core
        for c in range(2):
            ordered[2 * chip + (owner if c == 0 else 1 - owner)] = ref[c]
    for first in range(0, 2 * chips, group):
        base[:, first * width : (first + group) * width] = jnp.concatenate(
            [ordered[shard] for shard in range(first, first + group)], axis=1
        )
    copies = []
    for begin in range(0, out_ref.shape[1], sub):
        part = slice(begin, begin + sub)
        totals = []
        for s in range(2):
            right = jnp.concatenate(
                [noise_ref[s, :, part], base[s * seq : (s + 1) * seq, part]], axis=0
            )
            totals.append(jnp.dot(left_ref[s], right, preferred_element_type=jnp.float32))
        half = 0.5 * totals[0]
        buf[:, part] = ((half + half * jnp.tanh(half)) * totals[1]).astype(jnp.bfloat16)
        if (begin + sub) % chunk == 0:
            i = begin // chunk
            span = pl.ds(i * chunk, chunk)
            copies.append(
                pltpu.make_async_copy(buf.at[:, span], out_ref.at[:, span], sems.at[i])
            )
            copies[-1].start()
    for copy in copies:
        copy.wait()


def hidden_states(left, noise, shards, width, seq, sub=256, chunk=1536):
    rows = left.shape[1]
    total = noise.shape[2]
    return pl.pallas_call(
        functools.partial(hidden_kernel, seq=seq, sub=sub, chunk=chunk),
        out_shape=jax.ShapeDtypeStruct((rows, total), jnp.bfloat16),
        in_specs=[WHOLE] * (2 + len(shards)),
        out_specs=PLACED,
        scratch_shapes=[
            pltpu.VMEM((2 * len(shards), 2 * seq, width), jnp.bfloat16),
            pltpu.VMEM((2 * seq, total), jnp.bfloat16),
            pltpu.VMEM((rows, total), jnp.bfloat16),
            pltpu.SemaphoreType.DMA((total // chunk,)),
        ],
        compiler_params=room(16),
        cost_estimate=pl.CostEstimate(
            flops=10**8, bytes_accessed=6 * 10**6, transcendentals=2 * 10**6
        ),
        name="hidden",
    )(left, noise, *shards)


def columns_kernel(info_ref, got_ref, cols_ref, keys_ref, *, population):
    width, terms = cols_ref.shape[1:]
    norm = NOISE_SCALE * NOISE_SCALE / math.sqrt(population * R)
    info = info_ref[...] + got_ref[...]
    seeds = info[0:1, 0:population]
    ranks = info[1:2, 0:population]
    scale = ((ranks.astype(jnp.float32) + 0.5) / population - 0.5) * norm
    scales = jnp.concatenate([scale] * R, axis=1)
    wide = jnp.concatenate([seeds] * R, axis=1)
    for s in range(2):
        for t in range(0, population, 64):
            square = jnp.broadcast_to(seeds[:, t : t + 64].astype(jnp.float32), (128, 64))
            keys_ref[s, t : t + 64, :] = mixed(square.T.astype(jnp.int32) * 4 + 2 * s)
    lane_keys = [mixed(wide * 4 + (2 * s + 1)) for s in range(2)]
    part = width // 9
    offset = lax.axis_index("pop") * width

    def fill(r, carry):
        column = lax.broadcasted_iota(jnp.int32, (part, 128), 0) + (offset + r * part)
        lane = lax.broadcasted_iota(jnp.int32, (part, 128), 1)
        where = pl.ds(pl.multiple_of(r * part, 8), part)
        for t in range(0, terms, 128):
            hashes = mixed(column * R + (lane + t) // population + 1)
            for s in range(2):
                noise = centered(hashes ^ lane_keys[s][:, t : t + 128])
                cols_ref[s, where, t : t + 128] = (noise * scales[:, t : t + 128]).astype(jnp.bfloat16)
        return carry

    lax.fori_loop(0, 9, fill, 0)


def update_columns(info, got, population, width):
    return pl.pallas_call(
        functools.partial(columns_kernel, population=population),
        out_shape=(
            jax.ShapeDtypeStruct((2, width, population * R), jnp.bfloat16),
            jax.ShapeDtypeStruct((2, population, 128), jnp.int32),
        ),
        in_specs=[WHOLE, WHOLE],
        out_specs=(WHOLE, WHOLE),
        compiler_params=room(8),
        cost_estimate=pl.CostEstimate(flops=10**7, bytes_accessed=10**6, transcendentals=0),
        name="columns",
    )(info, got)


def update_kernel(keys_ref, cols_ref, out_ref, buf, rows_buf, sems, *, stream, sub, chunk):
    depth = out_ref.shape[1]
    population = keys_ref.shape[1]

    def generate(j):
        hashes = entries(j * sub, 8, sub)
        slot = j % 2
        for k in range(R):
            for q in range(0, sub, 128):
                entry = jnp.broadcast_to(hashes[k : k + 1, q : q + 128], (16, 128))
                for t in range(0, population, 16):
                    at = k * population + t
                    rows_buf[slot, at : at + 16, q : q + 128] = centered(
                        entry ^ keys_ref[stream, t : t + 16, :]
                    ).astype(jnp.bfloat16)

    count = depth // sub
    copies = []
    generate(0)
    for j in range(count):
        if j + 1 < count:
            generate(j + 1)
        buf[:, j * sub : (j + 1) * sub] = jnp.dot(
            cols_ref[stream], rows_buf[j % 2], preferred_element_type=jnp.float32
        ).astype(jnp.bfloat16)
        if (j + 1) * sub % chunk == 0:
            i = j * sub // chunk
            span = pl.ds(i * chunk, chunk)
            copies.append(
                pltpu.make_async_copy(buf.at[:, span], out_ref.at[:, span], sems.at[i])
            )
            copies[-1].start()
    for copy in copies:
        copy.wait()


def update(keys, cols, stream, depth, sub=256, chunk=512):
    width, terms = cols.shape[1:]
    return pl.pallas_call(
        functools.partial(update_kernel, stream=stream, sub=sub, chunk=chunk),
        out_shape=jax.ShapeDtypeStruct((width, depth), jnp.bfloat16),
        in_specs=[WHOLE, WHOLE],
        out_specs=PLACED,
        scratch_shapes=[
            pltpu.VMEM((width, depth), jnp.bfloat16),
            pltpu.VMEM((2, terms, sub), jnp.bfloat16),
            pltpu.SemaphoreType.DMA((depth // chunk,)),
        ],
        compiler_params=room(24),
        cost_estimate=pl.CostEstimate(
            flops=2 * width * terms * depth, bytes_accessed=2 * width * depth, transcendentals=0
        ),
        name="update",
    )(keys, cols)


def ring_order(chips):
    if chips <= 8:
        return list(range(0, chips, 2)) + list(range(chips - 1, 0, -2))
    return list(range(chips))


def together(*values):
    return lax.optimization_barrier(values)


def per_device(inputs, gate_weight, up_weight, member_seeds, member_ranks):
    devices = lax.axis_size("pop")
    depth, width = gate_weight.shape
    local = member_seeds.shape[0]
    seq = inputs.shape[0]
    population = devices * local
    chips = devices // 2
    order = ring_order(chips)
    siblings = [(i, i ^ 1) for i in range(devices)]
    onward = [
        (2 * order[i] + c, 2 * order[(i + 1 - 2 * c) % chips] + c) for i in range(chips) for c in range(2)
    ]

    base, info = base_projections(
        member_seeds, member_ranks, inputs, gate_weight.T, up_weight.T, -(-population // 128) * 128
    )
    got = lax.ppermute(info, "pop", siblings)
    sibling = lax.ppermute(base, "pop", siblings)
    left = left_operands(member_seeds, together(inputs, base)[0])
    info = info + got
    moving = jnp.stack([base, sibling])

    moving, info, left = together(moving, info, left)
    arrived, crossed = [moving], []
    stride = 2
    noise = cols = keys = None
    for k in range(1, chips // 2 + 1):
        onto = lax.ppermute(moving, "pop", onward)
        if stride < devices:
            got = lax.ppermute(info, "pop", [(i, i ^ stride) for i in range(devices)])
            stride *= 2
        if k > 1:
            crossed.append(lax.ppermute(moving, "pop", siblings))
        moving = onto
        arrived.append(moving)
        if k == 1:
            noise = output_noise(together(member_seeds, info)[0], devices * width)
            moving, noise = together(moving, noise)
        if cols is None:
            if stride < devices:
                info = info + got
                moving, info = together(moving, info)
            else:
                cols, keys = update_columns(info, got, population, width)
                moving, cols = together(moving, cols)
    first = update(keys, cols, 0, depth)
    second = update(keys, together(cols, first)[0], 1, depth)
    noise = together(noise, second)[0]
    hidden = hidden_states(left, noise, arrived + crossed, width, seq)
    return (hidden.reshape(local, seq, -1), first.T, second.T)


def solution(mesh):
    placed = (P("grp", None), P(None, "pop"), P(None, "pop"), P(("grp", "pop")), P(("grp", "pop")))
    return jax.shard_map(
        per_device,
        mesh=mesh,
        in_specs=placed,
        out_specs=(P(("grp", "pop"), None, None), P("grp", "pop"), P("grp", "pop")),
        check_vma=False,
    )
```

```python
import functools
import math

import jax
import jax.numpy as jnp
from jax import lax
from jax.experimental import pallas as pl
from jax.experimental.pallas import tpu as pltpu
from jax.sharding import PartitionSpec as P

R = 4
HASH_MULTIPLIER = 73244475
NOISE_SCALE = math.sqrt(3.0) / 32768.0
PERTURB = 0.3
MINOR = (((1,), (1,)), ((), ()))


def high(value):
    return lax.shift_right_logical(value, jnp.int32(16))


def scramble(value):
    value = (value ^ high(value)) * HASH_MULTIPLIER
    value = (value ^ high(value)) * HASH_MULTIPLIER
    return value ^ high(value)


def mixed(value):
    value = scramble(value)
    return value ^ high(value)


def centered(mix):
    value = mix * HASH_MULTIPLIER
    value = (value ^ high(value)) * HASH_MULTIPLIER
    return ((value ^ high(value)) & 65535).astype(jnp.float32) - 32767.5


def entries(start, rows, length):
    row = lax.broadcasted_iota(jnp.int32, (rows, length), 0)
    column = lax.broadcasted_iota(jnp.int32, (rows, length), 1) + start
    return mixed(column * R + (row & (R - 1)) + 1)


def own_keys(seeds_ref, stream, first):
    row = lax.broadcasted_iota(jnp.int32, (8, 128), 0)
    low = mixed(seeds_ref[first] * 4 + stream)
    top = mixed(seeds_ref[first + 1] * 4 + stream)
    return jnp.where(row < R, low, top)


def own_noise(seeds_ref, stream, hashes, length):
    pieces = []
    for first in range(0, seeds_ref.shape[0], 2):
        key = own_keys(seeds_ref, stream, first)
        pieces.append(
            jnp.concatenate(
                [centered(hashes[:, q : q + 128] ^ key) for q in range(0, length, 128)], axis=1
            )
        )
    return jnp.concatenate(pieces, axis=0).astype(jnp.bfloat16)


SCALARS = pl.BlockSpec(memory_space=pltpu.SMEM)
WHOLE = pl.BlockSpec(memory_space=pltpu.VMEM)
PLACED = pl.BlockSpec(memory_space=pl.ANY)
FULL_ROOM = 54


def room(mebibytes):
    return pltpu.CompilerParams(vmem_limit_bytes=mebibytes * 2**20)


def streamed_product(x, hbm, buf, sems, pieces, ahead):
    copies = []
    begin = 0
    for i, size in enumerate(pieces):
        part = pl.ds(begin, size)
        copies.append(pltpu.make_async_copy(hbm.at[:, part], buf.at[:, part], sems.at[i]))
        begin += size
    for copy in copies[:ahead]:
        copy.start()
    yield
    total = None
    begin = 0
    for i, size in enumerate(pieces):
        copies[i].wait()
        if i + ahead < len(pieces):
            copies[i + ahead].start()
        part = slice(begin, begin + size)
        term = lax.dot_general(x[:, part], buf[:, part], MINOR, preferred_element_type=jnp.float32)
        total = term if total is None else total + term
        begin += size
    yield total


def gate_kernel(
    seeds_ref, ranks_ref, x_ref, w_ref, out_ref, info_ref, own, x_buf, buf, small, sems, *, pieces, ahead
):
    first = [
        pltpu.make_async_copy(x_ref, x_buf, small.at[0]),
        pltpu.make_async_copy(seeds_ref, own.at[0], small.at[1]),
        pltpu.make_async_copy(ranks_ref, own.at[1], small.at[2]),
    ]
    for copy in first:
        copy.start()
    product = streamed_product(x_buf, w_ref, buf, sems, pieces, ahead)
    next(product)
    for copy in first:
        copy.wait()
    local = own.shape[1]
    row = lax.broadcasted_iota(jnp.int32, info_ref.shape, 0)
    lane = lax.broadcasted_iota(jnp.int32, info_ref.shape, 1) - lax.axis_index("pop") * local
    info = jnp.zeros(info_ref.shape, jnp.int32)
    for m in range(local):
        value = jnp.where(row == 0, own[0, m], jnp.where(row == 1, own[1, m], 0))
        info = jnp.where(lane == m, value, info)
    info_ref[...] = info
    out_ref[...] = next(product).astype(jnp.bfloat16)


def up_kernel(x_ref, gate_ref, w_ref, out_ref, buf, sems, *, pieces, ahead):
    seq = x_ref.shape[0]
    product = streamed_product(x_ref, w_ref, buf, sems, pieces, ahead)
    next(product)
    out_ref[0:seq] = gate_ref[...]
    out_ref[seq : 2 * seq] = next(product).astype(jnp.bfloat16)


def weight_pieces(depth):
    return (512,) + (1024,) * (depth // 1024 - 1) + (512,)


def gate_projection(seeds, ranks, inputs, rows, lanes):
    seq, depth = inputs.shape
    width = rows.shape[0]
    pieces = weight_pieces(depth)
    return pl.pallas_call(
        functools.partial(gate_kernel, pieces=pieces, ahead=4),
        out_shape=(
            jax.ShapeDtypeStruct((seq, width), jnp.bfloat16),
            jax.ShapeDtypeStruct((8, lanes), jnp.int32),
        ),
        in_specs=[PLACED] * 4,
        out_specs=(WHOLE, WHOLE),
        scratch_shapes=[
            pltpu.SMEM((2, seeds.shape[0]), jnp.int32),
            pltpu.VMEM((seq, depth), jnp.bfloat16),
            pltpu.VMEM((width, depth), jnp.bfloat16),
            pltpu.SemaphoreType.DMA((3,)),
            pltpu.SemaphoreType.DMA((len(pieces),)),
        ],
        compiler_params=room(FULL_ROOM),
        cost_estimate=pl.CostEstimate(
            flops=2 * seq * depth * width, bytes_accessed=2 * depth * width, transcendentals=0
        ),
        name="gate",
    )(seeds, ranks, inputs, rows)


def up_projection(inputs, gate, rows):
    seq, depth = inputs.shape
    width = rows.shape[0]
    pieces = weight_pieces(depth)
    return pl.pallas_call(
        functools.partial(up_kernel, pieces=pieces, ahead=4),
        out_shape=jax.ShapeDtypeStruct((2 * seq, width), jnp.bfloat16),
        in_specs=[WHOLE, WHOLE, PLACED],
        out_specs=WHOLE,
        scratch_shapes=[
            pltpu.VMEM((width, depth), jnp.bfloat16),
            pltpu.SemaphoreType.DMA((len(pieces),)),
        ],
        compiler_params=room(FULL_ROOM),
        cost_estimate=pl.CostEstimate(
            flops=2 * seq * depth * width, bytes_accessed=2 * depth * width, transcendentals=0
        ),
        name="up",
    )(inputs, gate, rows)


def coeff_kernel(seeds_ref, x_ref, out_ref):
    seq, depth = x_ref.shape
    members = seeds_ref.shape[0]
    rows = members * R
    scale = NOISE_SCALE / math.sqrt(depth) * (PERTURB / math.sqrt(R)) * NOISE_SCALE
    hashes = entries(0, 8, depth)
    x = x_ref[...]
    row = lax.broadcasted_iota(jnp.int32, (members * seq, rows + seq), 0)
    lane = lax.broadcasted_iota(jnp.int32, (members * seq, rows + seq), 1)
    own = (row // seq) == (lane // R)
    pick = (lane - rows) == (row % seq)
    for s in range(2):
        noise = own_noise(seeds_ref, 2 * s, hashes, depth)
        padded = jnp.concatenate([noise, jnp.zeros((seq, depth), jnp.bfloat16)], axis=0)
        coeff = lax.dot_general(x, padded, MINOR, preferred_element_type=jnp.float32) * scale
        tiled = jnp.concatenate([coeff] * members, axis=0)
        out_ref[s] = jnp.where(
            lane < rows, jnp.where(own, tiled, 0.0), jnp.where(pick, 1.0, 0.0)
        ).astype(jnp.bfloat16)


def left_operands(seeds, inputs):
    seq = inputs.shape[0]
    members = seeds.shape[0]
    return pl.pallas_call(
        coeff_kernel,
        out_shape=jax.ShapeDtypeStruct((2, members * seq, members * R + seq), jnp.bfloat16),
        in_specs=[SCALARS, WHOLE],
        out_specs=WHOLE,
        compiler_params=room(12),
        cost_estimate=pl.CostEstimate(flops=10**7, bytes_accessed=10**6, transcendentals=0),
        name="coeff",
    )(seeds, inputs)


def noise_kernel(seeds_ref, out_ref, *, part):
    for start in range(0, out_ref.shape[2], part):
        hashes = entries(start, 8, part)
        for s in range(2):
            out_ref[s, :, start : start + part] = own_noise(seeds_ref, 2 * s + 1, hashes, part)


def output_noise(seeds, total):
    return pl.pallas_call(
        functools.partial(noise_kernel, part=1536),
        out_shape=jax.ShapeDtypeStruct((2, seeds.shape[0] * R, total), jnp.bfloat16),
        in_specs=[SCALARS],
        out_specs=WHOLE,
        compiler_params=room(8),
        cost_estimate=pl.CostEstimate(flops=10**7, bytes_accessed=10**6, transcendentals=0),
        name="noise",
    )(seeds)


def chip_at(place, chips):
    if chips <= 8:
        return jnp.where(place < chips // 2, 2 * place, 2 * (chips - 1 - place) + 1)
    return place


def ring_place(chip, chips):
    if chips <= 8:
        return jnp.where(chip % 2 == 0, chip // 2, chips - 1 - chip // 2)
    return chip


def hidden_kernel(left_ref, noise_ref, *rest, seq, sub, chunk):
    shard_refs, (out_ref, ordered, base, buf, sems) = rest[:-5], rest[-5:]
    chips = len(shard_refs)
    reach = chips // 2
    width = base.shape[1] // (2 * chips)
    group = 128 // math.gcd(width, 128)
    position = lax.axis_index("pop")
    core = lax.rem(position, 2)
    here = ring_place(position // 2, chips)
    for i, ref in enumerate(shard_refs):
        step = i if i <= reach else i - reach
        toward = 2 * core - 1 if i <= reach else 1 - 2 * core
        chip = chip_at(lax.rem(here + toward * step + chips, chips), chips)
        owner = core if i <= reach else 1 - core
        for c in range(2):
            ordered[2 * chip + (owner if c == 0 else 1 - owner)] = ref[c]
    for first in range(0, 2 * chips, group):
        base[:, first * width : (first + group) * width] = jnp.concatenate(
            [ordered[shard] for shard in range(first, first + group)], axis=1
        )
    copies = []
    for begin in range(0, out_ref.shape[1], sub):
        part = slice(begin, begin + sub)
        totals = []
        for s in range(2):
            right = jnp.concatenate(
                [noise_ref[s, :, part], base[s * seq : (s + 1) * seq, part]], axis=0
            )
            totals.append(jnp.dot(left_ref[s], right, preferred_element_type=jnp.float32))
        half = 0.5 * totals[0]
        buf[:, part] = ((half + half * jnp.tanh(half)) * totals[1]).astype(jnp.bfloat16)
        if (begin + sub) % chunk == 0:
            i = begin // chunk
            span = pl.ds(i * chunk, chunk)
            copies.append(
                pltpu.make_async_copy(buf.at[:, span], out_ref.at[:, span], sems.at[i])
            )
            copies[-1].start()
    for copy in copies:
        copy.wait()


def hidden_states(left, noise, shards, width, seq, sub=256, chunk=1536):
    rows = left.shape[1]
    total = noise.shape[2]
    return pl.pallas_call(
        functools.partial(hidden_kernel, seq=seq, sub=sub, chunk=chunk),
        out_shape=jax.ShapeDtypeStruct((rows, total), jnp.bfloat16),
        in_specs=[WHOLE] * (2 + len(shards)),
        out_specs=PLACED,
        scratch_shapes=[
            pltpu.VMEM((2 * len(shards), 2 * seq, width), jnp.bfloat16),
            pltpu.VMEM((2 * seq, total), jnp.bfloat16),
            pltpu.VMEM((rows, total), jnp.bfloat16),
            pltpu.SemaphoreType.DMA((total // chunk,)),
        ],
        compiler_params=room(16),
        cost_estimate=pl.CostEstimate(
            flops=10**8, bytes_accessed=6 * 10**6, transcendentals=2 * 10**6
        ),
        name="hidden",
    )(left, noise, *shards)


def columns_kernel(info_ref, got_ref, cols_ref, keys_ref, *, population):
    width, terms = cols_ref.shape[1:]
    norm = NOISE_SCALE * NOISE_SCALE / math.sqrt(population * R)
    info = info_ref[...] + got_ref[...]
    seeds = info[0:1, 0:population]
    ranks = info[1:2, 0:population]
    scale = ((ranks.astype(jnp.float32) + 0.5) / population - 0.5) * norm
    scales = jnp.concatenate([scale] * R, axis=1)
    wide = jnp.concatenate([seeds] * R, axis=1)
    for s in range(2):
        for t in range(0, population, 64):
            square = jnp.broadcast_to(seeds[:, t : t + 64].astype(jnp.float32), (128, 64))
            keys_ref[s, t : t + 64, :] = mixed(square.T.astype(jnp.int32) * 4 + 2 * s)
    lane_keys = [mixed(wide * 4 + (2 * s + 1)) for s in range(2)]
    part = width // 9
    offset = lax.axis_index("pop") * width

    def fill(r, carry):
        column = lax.broadcasted_iota(jnp.int32, (part, 128), 0) + (offset + r * part)
        lane = lax.broadcasted_iota(jnp.int32, (part, 128), 1)
        where = pl.ds(pl.multiple_of(r * part, 8), part)
        for t in range(0, terms, 128):
            hashes = mixed(column * R + (lane + t) // population + 1)
            for s in range(2):
                noise = centered(hashes ^ lane_keys[s][:, t : t + 128])
                cols_ref[s, where, t : t + 128] = (noise * scales[:, t : t + 128]).astype(jnp.bfloat16)
        return carry

    lax.fori_loop(0, 9, fill, 0)


def update_columns(info, got, population, width):
    return pl.pallas_call(
        functools.partial(columns_kernel, population=population),
        out_shape=(
            jax.ShapeDtypeStruct((2, width, population * R), jnp.bfloat16),
            jax.ShapeDtypeStruct((2, population, 128), jnp.int32),
        ),
        in_specs=[WHOLE, WHOLE],
        out_specs=(WHOLE, WHOLE),
        compiler_params=room(8),
        cost_estimate=pl.CostEstimate(flops=10**7, bytes_accessed=10**6, transcendentals=0),
        name="columns",
    )(info, got)


def update_kernel(keys_ref, cols_ref, *rest, stream, start, sub, chunk):
    out_ref, buf, rows_buf, sems = rest[-4:]
    extent = buf.shape[1]
    population = keys_ref.shape[1]

    def generate(j):
        hashes = entries(start + j * sub, 8, sub)
        slot = j % 2
        for k in range(R):
            for q in range(0, sub, 128):
                entry = jnp.broadcast_to(hashes[k : k + 1, q : q + 128], (16, 128))
                for t in range(0, population, 16):
                    at = k * population + t
                    rows_buf[slot, at : at + 16, q : q + 128] = centered(
                        entry ^ keys_ref[stream, t : t + 16, :]
                    ).astype(jnp.bfloat16)

    count = extent // sub
    copies = []
    generate(0)
    for j in range(count):
        if j + 1 < count:
            generate(j + 1)
        buf[:, j * sub : (j + 1) * sub] = jnp.dot(
            cols_ref[stream], rows_buf[j % 2], preferred_element_type=jnp.float32
        ).astype(jnp.bfloat16)
        if (j + 1) * sub % chunk == 0:
            i = j * sub // chunk
            copies.append(
                pltpu.make_async_copy(
                    buf.at[:, pl.ds(i * chunk, chunk)],
                    out_ref.at[:, pl.ds(start + i * chunk, chunk)],
                    sems.at[i],
                )
            )
            copies[-1].start()
    for copy in copies:
        copy.wait()


def update(keys, cols, stream, depth, piece=0, pieces=1, onto=None, sub=256, chunk=512):
    width, terms = cols.shape[1:]
    extent = depth // pieces
    return pl.pallas_call(
        functools.partial(update_kernel, stream=stream, start=piece * extent, sub=sub, chunk=chunk),
        out_shape=jax.ShapeDtypeStruct((width, depth), jnp.bfloat16),
        in_specs=[WHOLE, WHOLE] + ([] if onto is None else [PLACED]),
        out_specs=PLACED,
        scratch_shapes=[
            pltpu.VMEM((width, extent), jnp.bfloat16),
            pltpu.VMEM((2, terms, sub), jnp.bfloat16),
            pltpu.SemaphoreType.DMA((extent // chunk,)),
        ],
        input_output_aliases={} if onto is None else {2: 0},
        compiler_params=room(24),
        cost_estimate=pl.CostEstimate(
            flops=2 * width * terms * extent, bytes_accessed=2 * width * extent, transcendentals=0
        ),
        name="update",
    )(keys, cols, *(() if onto is None else (onto,)))


def ring_order(chips):
    if chips <= 8:
        return list(range(0, chips, 2)) + list(range(chips - 1, 0, -2))
    return list(range(chips))


def together(*values):
    return lax.optimization_barrier(values)


def per_device(inputs, gate_weight, up_weight, member_seeds, member_ranks):
    devices = lax.axis_size("pop")
    depth, width = gate_weight.shape
    local = member_seeds.shape[0]
    seq = inputs.shape[0]
    population = devices * local
    chips = devices // 2
    order = ring_order(chips)
    siblings = [(i, i ^ 1) for i in range(devices)]
    onward = [
        (2 * order[i] + c, 2 * order[(i + 1 - 2 * c) % chips] + c) for i in range(chips) for c in range(2)
    ]

    lanes = -(-population // 128) * 128
    gate, info = gate_projection(member_seeds, member_ranks, inputs, gate_weight.T, lanes)
    got = lax.ppermute(info, "pop", siblings)
    base = up_projection(together(inputs, info)[0], gate, up_weight.T)
    stride = 2

    def seed_step(info, stride):
        return lax.ppermute(info, "pop", [(i, i ^ stride) for i in range(devices)])

    base, info = together(base, info + got)
    got = seed_step(info, stride)
    sibling = lax.ppermute(base, "pop", siblings)
    left = left_operands(member_seeds, together(inputs, base)[0])
    info, base, sibling, left = together(info + got, base, sibling, left)
    stride *= 2
    got = seed_step(info, stride)
    moving = jnp.stack([base, sibling])
    arrived, crossed = [moving], []
    cols = keys = None
    noise = output_noise(together(member_seeds, moving)[0], devices * width)
    updates = [None, None]
    work = [[], [(0, 0)], [(0, 1), (1, 0)], [(1, 1)]]
    steps = chips // 2
    for k in range(1, steps + 1):
        onto = lax.ppermute(moving, "pop", onward)
        if k > 1:
            crossed.append(lax.ppermute(moving, "pop", siblings))
        if k == 1:
            onto, noise = together(onto, noise)
        if cols is None:
            stride *= 2
            info = info + got
            got = seed_step(info, stride)
            if 2 * stride == devices:
                info, got, onto = together(info, got, onto)
                cols, keys = update_columns(info, got, population, width)
            pieces = work.pop(0)
        else:
            pieces = work.pop(0) if work else []
        moving = onto
        arrived.append(moving)
        for s, piece in pieces:
            updates[s] = update(keys, cols, s, depth, piece, 2, updates[s])
            cols = together(cols, updates[s])[0]
        if pieces and work:
            moving, cols = together(moving, cols)
        if cols is None:
            work.insert(0, [])
    noise = together(noise, *updates)[0]
    hidden = hidden_states(left, noise, arrived + crossed, width, seq)
    return (hidden.reshape(local, seq, -1), updates[0].T, updates[1].T)


def solution(mesh):
    placed = (P("grp", None), P(None, "pop"), P(None, "pop"), P(("grp", "pop")), P(("grp", "pop")))
    return jax.shard_map(
        per_device,
        mesh=mesh,
        in_specs=placed,
        out_specs=(P(("grp", "pop"), None, None), P("grp", "pop"), P("grp", "pop")),
        check_vma=False,
    )
```

```python
import functools
import math

import jax
import jax.numpy as jnp
from jax import lax
from jax.experimental import pallas as pl
from jax.experimental.pallas import tpu as pltpu
from jax.sharding import PartitionSpec as P


R = 4
HASH_MULTIPLIER = 73244475
NOISE_SCALE = math.sqrt(3.0) / 32768.0
PERTURB = 0.3
MINOR = (((1,), (1,)), ((), ()))


def high(value):
    return lax.shift_right_logical(value, jnp.int32(16))


def scramble(value):
    value = (value ^ high(value)) * HASH_MULTIPLIER
    value = (value ^ high(value)) * HASH_MULTIPLIER
    return value ^ high(value)


def mixed(value):
    value = scramble(value)
    return value ^ high(value)


def centered(mix):
    value = mix * HASH_MULTIPLIER
    value = (value ^ high(value)) * HASH_MULTIPLIER
    return ((value ^ high(value)) & 65535).astype(jnp.float32) - 32767.5


def entries(start, rows, length):
    row = lax.broadcasted_iota(jnp.int32, (rows, length), 0)
    column = lax.broadcasted_iota(jnp.int32, (rows, length), 1) + start
    return mixed(column * R + (row & (R - 1)) + 1)


def own_keys(seeds_ref, stream, first):
    row = lax.broadcasted_iota(jnp.int32, (8, 128), 0)
    low = mixed(seeds_ref[first] * 4 + stream)
    top = mixed(seeds_ref[first + 1] * 4 + stream)
    return jnp.where(row < R, low, top)


def own_noise(seeds_ref, stream, hashes, length):
    pieces = []
    for first in range(0, seeds_ref.shape[0], 2):
        key = own_keys(seeds_ref, stream, first)
        pieces.append(
            jnp.concatenate(
                [centered(hashes[:, q : q + 128] ^ key) for q in range(0, length, 128)], axis=1
            )
        )
    return jnp.concatenate(pieces, axis=0).astype(jnp.bfloat16)


SCALARS = pl.BlockSpec(memory_space=pltpu.SMEM)
WHOLE = pl.BlockSpec(memory_space=pltpu.VMEM)
PLACED = pl.BlockSpec(memory_space=pl.ANY)


def room(mebibytes):
    return pltpu.CompilerParams(vmem_limit_bytes=mebibytes * 2**20)


def base_kernel(
    seeds_ref, ranks_ref, x_ref, gate_ref, up_ref, out_ref, info_ref, own, x_buf, gate_buf, up_buf, small, sems, *, pieces, ahead
):
    seq = x_buf.shape[0]
    first = [
        pltpu.make_async_copy(x_ref, x_buf, small.at[0]),
        pltpu.make_async_copy(seeds_ref, own.at[0], small.at[1]),
        pltpu.make_async_copy(ranks_ref, own.at[1], small.at[2]),
    ]
    copies = []
    begin = 0
    for i, size in enumerate(pieces):
        part = pl.ds(begin, size)
        copies.append(
            (
                pltpu.make_async_copy(gate_ref.at[:, part], gate_buf.at[:, part], sems.at[0, i]),
                pltpu.make_async_copy(up_ref.at[:, part], up_buf.at[:, part], sems.at[1, i]),
            )
        )
        begin += size
    for copy in first:
        copy.start()
    for pair in copies[:ahead]:
        for copy in pair:
            copy.start()
    for copy in first:
        copy.wait()
    local = own.shape[1]
    row = lax.broadcasted_iota(jnp.int32, info_ref.shape, 0)
    lane = lax.broadcasted_iota(jnp.int32, info_ref.shape, 1) - lax.axis_index("pop") * local
    info = jnp.zeros(info_ref.shape, jnp.int32)
    for m in range(local):
        value = jnp.where(row == 0, own[0, m], jnp.where(row == 1, own[1, m], 0))
        info = jnp.where(lane == m, value, info)
    info_ref[...] = info
    sums = [None, None]
    begin = 0
    for i, size in enumerate(pieces):
        for copy in copies[i]:
            copy.wait()
        if i + ahead < len(pieces):
            for copy in copies[i + ahead]:
                copy.start()
        part = slice(begin, begin + size)
        for s, buf in enumerate((gate_buf, up_buf)):
            term = lax.dot_general(
                x_buf[:, part], buf[:, part], MINOR, preferred_element_type=jnp.float32
            )
            sums[s] = term if sums[s] is None else sums[s] + term
        begin += size
    for s in range(2):
        out_ref[s * seq : (s + 1) * seq] = sums[s].astype(jnp.bfloat16)


def base_projections(seeds, ranks, inputs, gate_rows, up_rows, lanes):
    seq, depth = inputs.shape
    width = gate_rows.shape[0]
    pieces = (512,) + (1024,) * (depth // 1024 - 1) + (512,)
    return pl.pallas_call(
        functools.partial(base_kernel, pieces=pieces, ahead=3),
        out_shape=(
            jax.ShapeDtypeStruct((2 * seq, width), jnp.bfloat16),
            jax.ShapeDtypeStruct((8, lanes), jnp.int32),
        ),
        in_specs=[PLACED] * 5,
        out_specs=(WHOLE, WHOLE),
        scratch_shapes=[
            pltpu.SMEM((2, seeds.shape[0]), jnp.int32),
            pltpu.VMEM((seq, depth), jnp.bfloat16),
            pltpu.VMEM((width, depth), jnp.bfloat16),
            pltpu.VMEM((width, depth), jnp.bfloat16),
            pltpu.SemaphoreType.DMA((3,)),
            pltpu.SemaphoreType.DMA((2, len(pieces))),
        ],
        compiler_params=room(57),
        cost_estimate=pl.CostEstimate(
            flops=4 * seq * depth * width, bytes_accessed=4 * depth * width, transcendentals=0
        ),
        name="base",
    )(seeds, ranks, inputs, gate_rows, up_rows)


def coeff_kernel(seeds_ref, x_ref, out_ref):
    seq, depth = x_ref.shape
    members = seeds_ref.shape[0]
    rows = members * R
    scale = NOISE_SCALE / math.sqrt(depth) * (PERTURB / math.sqrt(R)) * NOISE_SCALE
    hashes = entries(0, 8, depth)
    x = x_ref[...]
    row = lax.broadcasted_iota(jnp.int32, (members * seq, rows + seq), 0)
    lane = lax.broadcasted_iota(jnp.int32, (members * seq, rows + seq), 1)
    own = (row // seq) == (lane // R)
    pick = (lane - rows) == (row % seq)
    for s in range(2):
        noise = own_noise(seeds_ref, 2 * s, hashes, depth)
        padded = jnp.concatenate([noise, jnp.zeros((seq, depth), jnp.bfloat16)], axis=0)
        coeff = lax.dot_general(x, padded, MINOR, preferred_element_type=jnp.float32) * scale
        tiled = jnp.concatenate([coeff] * members, axis=0)
        out_ref[s] = jnp.where(
            lane < rows, jnp.where(own, tiled, 0.0), jnp.where(pick, 1.0, 0.0)
        ).astype(jnp.bfloat16)


def left_operands(seeds, inputs):
    seq = inputs.shape[0]
    members = seeds.shape[0]
    return pl.pallas_call(
        coeff_kernel,
        out_shape=jax.ShapeDtypeStruct((2, members * seq, members * R + seq), jnp.bfloat16),
        in_specs=[SCALARS, WHOLE],
        out_specs=WHOLE,
        compiler_params=room(12),
        cost_estimate=pl.CostEstimate(flops=10**7, bytes_accessed=10**6, transcendentals=0),
        name="coeff",
    )(seeds, inputs)


def noise_kernel(seeds_ref, out_ref, *, part):
    for start in range(0, out_ref.shape[2], part):
        hashes = entries(start, 8, part)
        for s in range(2):
            out_ref[s, :, start : start + part] = own_noise(seeds_ref, 2 * s + 1, hashes, part)


def output_noise(seeds, total):
    return pl.pallas_call(
        functools.partial(noise_kernel, part=1536),
        out_shape=jax.ShapeDtypeStruct((2, seeds.shape[0] * R, total), jnp.bfloat16),
        in_specs=[SCALARS],
        out_specs=WHOLE,
        compiler_params=room(8),
        cost_estimate=pl.CostEstimate(flops=10**7, bytes_accessed=10**6, transcendentals=0),
        name="noise",
    )(seeds)


def chip_at(place, chips):
    if chips <= 8:
        return jnp.where(place < chips // 2, 2 * place, 2 * (chips - 1 - place) + 1)
    return place


def ring_place(chip, chips):
    if chips <= 8:
        return jnp.where(chip % 2 == 0, chip // 2, chips - 1 - chip // 2)
    return chip


def hidden_kernel(left_ref, noise_ref, *rest, seq, sub, chunk):
    shard_refs, (out_ref, ordered, base, buf, sems) = rest[:-5], rest[-5:]
    chips = len(shard_refs)
    reach = chips // 2
    width = base.shape[1] // (2 * chips)
    group = 128 // math.gcd(width, 128)
    position = lax.axis_index("pop")
    core = lax.rem(position, 2)
    here = ring_place(position // 2, chips)
    for i, ref in enumerate(shard_refs):
        step = i if i <= reach else i - reach
        toward = 2 * core - 1 if i <= reach else 1 - 2 * core
        chip = chip_at(lax.rem(here + toward * step + chips, chips), chips)
        owner = core if i <= reach else 1 - core
        for c in range(2):
            ordered[2 * chip + (owner if c == 0 else 1 - owner)] = ref[c]
    for first in range(0, 2 * chips, group):
        base[:, first * width : (first + group) * width] = jnp.concatenate(
            [ordered[shard] for shard in range(first, first + group)], axis=1
        )
    copies = []
    for begin in range(0, out_ref.shape[1], sub):
        part = slice(begin, begin + sub)
        totals = []
        for s in range(2):
            right = jnp.concatenate(
                [noise_ref[s, :, part], base[s * seq : (s + 1) * seq, part]], axis=0
            )
            totals.append(jnp.dot(left_ref[s], right, preferred_element_type=jnp.float32))
        half = 0.5 * totals[0]
        buf[:, part] = ((half + half * jnp.tanh(half)) * totals[1]).astype(jnp.bfloat16)
        if (begin + sub) % chunk == 0:
            i = begin // chunk
            span = pl.ds(i * chunk, chunk)
            copies.append(
                pltpu.make_async_copy(buf.at[:, span], out_ref.at[:, span], sems.at[i])
            )
            copies[-1].start()
    for copy in copies:
        copy.wait()


def hidden_states(left, noise, shards, width, seq, sub=256, chunk=1536):
    rows = left.shape[1]
    total = noise.shape[2]
    return pl.pallas_call(
        functools.partial(hidden_kernel, seq=seq, sub=sub, chunk=chunk),
        out_shape=jax.ShapeDtypeStruct((rows, total), jnp.bfloat16),
        in_specs=[WHOLE] * (2 + len(shards)),
        out_specs=PLACED,
        scratch_shapes=[
            pltpu.VMEM((2 * len(shards), 2 * seq, width), jnp.bfloat16),
            pltpu.VMEM((2 * seq, total), jnp.bfloat16),
            pltpu.VMEM((rows, total), jnp.bfloat16),
            pltpu.SemaphoreType.DMA((total // chunk,)),
        ],
        compiler_params=room(16),
        cost_estimate=pl.CostEstimate(
            flops=10**8, bytes_accessed=6 * 10**6, transcendentals=2 * 10**6
        ),
        name="hidden",
    )(left, noise, *shards)


def columns_kernel(info_ref, got_ref, cols_ref, keys_ref, *, population):
    width, terms = cols_ref.shape[1:]
    norm = NOISE_SCALE * NOISE_SCALE / math.sqrt(population * R)
    info = info_ref[...] + got_ref[...]
    seeds = info[0:1, 0:population]
    ranks = info[1:2, 0:population]
    scale = ((ranks.astype(jnp.float32) + 0.5) / population - 0.5) * norm
    scales = jnp.concatenate([scale] * R, axis=1)
    wide = jnp.concatenate([seeds] * R, axis=1)
    for s in range(2):
        for t in range(0, population, 64):
            square = jnp.broadcast_to(seeds[:, t : t + 64].astype(jnp.float32), (128, 64))
            keys_ref[s, t : t + 64, :] = mixed(square.T.astype(jnp.int32) * 4 + 2 * s)
    lane_keys = [mixed(wide * 4 + (2 * s + 1)) for s in range(2)]
    part = width // 9
    offset = lax.axis_index("pop") * width

    def fill(r, carry):
        column = lax.broadcasted_iota(jnp.int32, (part, 128), 0) + (offset + r * part)
        lane = lax.broadcasted_iota(jnp.int32, (part, 128), 1)
        where = pl.ds(pl.multiple_of(r * part, 8), part)
        for t in range(0, terms, 128):
            hashes = mixed(column * R + (lane + t) // population + 1)
            for s in range(2):
                noise = centered(hashes ^ lane_keys[s][:, t : t + 128])
                cols_ref[s, where, t : t + 128] = (noise * scales[:, t : t + 128]).astype(jnp.bfloat16)
        return carry

    lax.fori_loop(0, 9, fill, 0)


def update_columns(info, got, population, width):
    return pl.pallas_call(
        functools.partial(columns_kernel, population=population),
        out_shape=(
            jax.ShapeDtypeStruct((2, width, population * R), jnp.bfloat16),
            jax.ShapeDtypeStruct((2, population, 128), jnp.int32),
        ),
        in_specs=[WHOLE, WHOLE],
        out_specs=(WHOLE, WHOLE),
        compiler_params=room(8),
        cost_estimate=pl.CostEstimate(flops=10**7, bytes_accessed=10**6, transcendentals=0),
        name="columns",
    )(info, got)


def update_kernel(keys_ref, cols_ref, out_ref, buf, rows_buf, sems, *, stream, sub, chunk):
    depth = out_ref.shape[1]
    population = keys_ref.shape[1]

    def generate(j):
        hashes = entries(j * sub, 8, sub)
        slot = j % 2
        for k in range(R):
            for q in range(0, sub, 128):
                entry = jnp.broadcast_to(hashes[k : k + 1, q : q + 128], (16, 128))
                for t in range(0, population, 16):
                    at = k * population + t
                    rows_buf[slot, at : at + 16, q : q + 128] = centered(
                        entry ^ keys_ref[stream, t : t + 16, :]
                    ).astype(jnp.bfloat16)

    count = depth // sub
    copies = []
    generate(0)
    for j in range(count):
        if j + 1 < count:
            generate(j + 1)
        buf[:, j * sub : (j + 1) * sub] = jnp.dot(
            cols_ref[stream], rows_buf[j % 2], preferred_element_type=jnp.float32
        ).astype(jnp.bfloat16)
        if (j + 1) * sub % chunk == 0:
            i = j * sub // chunk
            span = pl.ds(i * chunk, chunk)
            copies.append(
                pltpu.make_async_copy(buf.at[:, span], out_ref.at[:, span], sems.at[i])
            )
            copies[-1].start()
    for copy in copies:
        copy.wait()


def update(keys, cols, stream, depth, sub=256, chunk=512):
    width, terms = cols.shape[1:]
    return pl.pallas_call(
        functools.partial(update_kernel, stream=stream, sub=sub, chunk=chunk),
        out_shape=jax.ShapeDtypeStruct((width, depth), jnp.bfloat16),
        in_specs=[WHOLE, WHOLE],
        out_specs=PLACED,
        scratch_shapes=[
            pltpu.VMEM((width, depth), jnp.bfloat16),
            pltpu.VMEM((2, terms, sub), jnp.bfloat16),
            pltpu.SemaphoreType.DMA((depth // chunk,)),
        ],
        compiler_params=room(24),
        cost_estimate=pl.CostEstimate(
            flops=2 * width * terms * depth, bytes_accessed=2 * width * depth, transcendentals=0
        ),
        name="update",
    )(keys, cols)


def ring_order(chips):
    if chips <= 8:
        return list(range(0, chips, 2)) + list(range(chips - 1, 0, -2))
    return list(range(chips))


def together(*values):
    return lax.optimization_barrier(values)


def per_device(inputs, gate_weight, up_weight, member_seeds, member_ranks):
    devices = lax.axis_size("pop")
    depth, width = gate_weight.shape
    local = member_seeds.shape[0]
    seq = inputs.shape[0]
    population = devices * local
    chips = devices // 2
    order = ring_order(chips)
    siblings = [(i, i ^ 1) for i in range(devices)]
    onward = [
        (2 * order[i] + c, 2 * order[(i + 1 - 2 * c) % chips] + c) for i in range(chips) for c in range(2)
    ]

    base, info = base_projections(
        member_seeds, member_ranks, inputs, gate_weight.T, up_weight.T, -(-population // 128) * 128
    )

    def named(value, pairs):
        return lax.ppermute(value, "pop", pairs)

    def seed_step(info, stride):
        return named(info, [(i, i ^ stride) for i in range(devices)])

    got = seed_step(info, 1)
    sibling = lax.ppermute(base, "pop", siblings)
    left = left_operands(member_seeds, together(inputs, base)[0])
    info, base, sibling, left = together(info + got, base, sibling, left)
    stride = 2
    got = seed_step(info, stride)
    moving = jnp.stack([base, sibling])
    arrived, crossed = [moving], []
    noise = output_noise(together(member_seeds, moving)[0], devices * width)
    cols = keys = None
    updates = [None, None]
    for k in range(1, chips // 2 + 1):
        onto = named(moving, onward)
        if k == 1:
            onto, noise = together(onto, noise)
        else:
            crossed.append(lax.ppermute(moving, "pop", siblings))
        if cols is None and 2 * stride < devices:
            info = info + got
            stride *= 2
            got = seed_step(info, stride)
        elif cols is None:
            cols, keys = update_columns(*together(info, got, moving)[:2], population, width)
            updates[0] = update(keys, cols, 0, depth)
            onto, cols, first = together(onto, cols, updates[0])
            updates[0] = first
        elif updates[1] is None:
            updates[1] = update(keys, cols, 1, depth)
        moving = onto
        arrived.append(moving)
    noise = together(noise, *updates)[0]
    hidden = hidden_states(left, noise, arrived + crossed, width, seq)
    return (hidden.reshape(local, seq, -1), updates[0].T, updates[1].T)


def solution(mesh):
    placed = (P("grp", None), P(None, "pop"), P(None, "pop"), P(("grp", "pop")), P(("grp", "pop")))
    return jax.shard_map(
        per_device,
        mesh=mesh,
        in_specs=placed,
        out_specs=(P(("grp", "pop"), None, None), P("grp", "pop"), P("grp", "pop")),
        check_vma=False,
    )
```

```python
import functools
import math

import jax
import jax.numpy as jnp
from jax import lax
from jax.experimental import pallas as pl
from jax.experimental.pallas import tpu as pltpu
from jax.sharding import PartitionSpec as P


R = 4
HASH_MULTIPLIER = 73244475
NOISE_SCALE = math.sqrt(3.0) / 32768.0
PERTURB = 0.3
MINOR = (((1,), (1,)), ((), ()))


def high(value):
    return lax.shift_right_logical(value, jnp.int32(16))


def scramble(value):
    value = (value ^ high(value)) * HASH_MULTIPLIER
    value = (value ^ high(value)) * HASH_MULTIPLIER
    return value ^ high(value)


def mixed(value):
    value = scramble(value)
    return value ^ high(value)


def centered(mix):
    value = mix * HASH_MULTIPLIER
    value = (value ^ high(value)) * HASH_MULTIPLIER
    return ((value ^ high(value)) & 65535).astype(jnp.float32) - 32767.5


def entries(start, rows, length):
    row = lax.broadcasted_iota(jnp.int32, (rows, length), 0)
    column = lax.broadcasted_iota(jnp.int32, (rows, length), 1) + start
    return mixed(column * R + (row & (R - 1)) + 1)


def own_keys(seeds_ref, stream, first):
    row = lax.broadcasted_iota(jnp.int32, (8, 128), 0)
    low = mixed(seeds_ref[first] * 4 + stream)
    top = mixed(seeds_ref[first + 1] * 4 + stream)
    return jnp.where(row < R, low, top)


def own_noise(seeds_ref, stream, hashes, length):
    pieces = []
    for first in range(0, seeds_ref.shape[0], 2):
        key = own_keys(seeds_ref, stream, first)
        pieces.append(
            jnp.concatenate(
                [centered(hashes[:, q : q + 128] ^ key) for q in range(0, length, 128)], axis=1
            )
        )
    return jnp.concatenate(pieces, axis=0).astype(jnp.bfloat16)


SCALARS = pl.BlockSpec(memory_space=pltpu.SMEM)
WHOLE = pl.BlockSpec(memory_space=pltpu.VMEM)
PLACED = pl.BlockSpec(memory_space=pl.ANY)


def room(mebibytes):
    return pltpu.CompilerParams(vmem_limit_bytes=mebibytes * 2**20)


def base_kernel(
    seeds_ref, ranks_ref, x_ref, gate_ref, up_ref, out_ref, info_ref, own, x_buf, gate_buf, up_buf, small, sems, *, pieces, ahead
):
    seq = x_buf.shape[0]
    first = [
        pltpu.make_async_copy(x_ref, x_buf, small.at[0]),
        pltpu.make_async_copy(seeds_ref, own.at[0], small.at[1]),
        pltpu.make_async_copy(ranks_ref, own.at[1], small.at[2]),
    ]
    copies = []
    begin = 0
    for i, size in enumerate(pieces):
        part = pl.ds(begin, size)
        copies.append(
            (
                pltpu.make_async_copy(gate_ref.at[:, part], gate_buf.at[:, part], sems.at[0, i]),
                pltpu.make_async_copy(up_ref.at[:, part], up_buf.at[:, part], sems.at[1, i]),
            )
        )
        begin += size
    for copy in first:
        copy.start()
    for pair in copies[:ahead]:
        for copy in pair:
            copy.start()
    for copy in first:
        copy.wait()
    local = own.shape[1]
    row = lax.broadcasted_iota(jnp.int32, info_ref.shape, 0)
    lane = lax.broadcasted_iota(jnp.int32, info_ref.shape, 1) - lax.axis_index("pop") * local
    info = jnp.zeros(info_ref.shape, jnp.int32)
    for m in range(local):
        value = jnp.where(row == 0, own[0, m], jnp.where(row == 1, own[1, m], 0))
        info = jnp.where(lane == m, value, info)
    info_ref[...] = info
    sums = [None, None]
    begin = 0
    for i, size in enumerate(pieces):
        for copy in copies[i]:
            copy.wait()
        if i + ahead < len(pieces):
            for copy in copies[i + ahead]:
                copy.start()
        part = slice(begin, begin + size)
        for s, buf in enumerate((gate_buf, up_buf)):
            term = lax.dot_general(
                x_buf[:, part], buf[:, part], MINOR, preferred_element_type=jnp.float32
            )
            sums[s] = term if sums[s] is None else sums[s] + term
        begin += size
    for s in range(2):
        out_ref[s * seq : (s + 1) * seq] = sums[s].astype(jnp.bfloat16)


def base_projections(seeds, ranks, inputs, gate_rows, up_rows, lanes):
    seq, depth = inputs.shape
    width = gate_rows.shape[0]
    pieces = (512,) + (1024,) * (depth // 1024 - 1) + (512,)
    return pl.pallas_call(
        functools.partial(base_kernel, pieces=pieces, ahead=3),
        out_shape=(
            jax.ShapeDtypeStruct((2 * seq, width), jnp.bfloat16),
            jax.ShapeDtypeStruct((8, lanes), jnp.int32),
        ),
        in_specs=[PLACED] * 5,
        out_specs=(WHOLE, WHOLE),
        scratch_shapes=[
            pltpu.SMEM((2, seeds.shape[0]), jnp.int32),
            pltpu.VMEM((seq, depth), jnp.bfloat16),
            pltpu.VMEM((width, depth), jnp.bfloat16),
            pltpu.VMEM((width, depth), jnp.bfloat16),
            pltpu.SemaphoreType.DMA((3,)),
            pltpu.SemaphoreType.DMA((2, len(pieces))),
        ],
        compiler_params=room(57),
        cost_estimate=pl.CostEstimate(
            flops=4 * seq * depth * width, bytes_accessed=4 * depth * width, transcendentals=0
        ),
        name="base",
    )(seeds, ranks, inputs, gate_rows, up_rows)


def coeff_kernel(seeds_ref, x_ref, base_ref, info_ref, out_ref, pair_ref, kept_ref):
    seq, depth = x_ref.shape
    members = seeds_ref.shape[0]
    rows = members * R
    pair_ref[0] = base_ref[...]
    pair_ref[1] = base_ref[...]
    kept_ref[...] = info_ref[...]
    scale = NOISE_SCALE / math.sqrt(depth) * (PERTURB / math.sqrt(R)) * NOISE_SCALE
    hashes = entries(0, 8, depth)
    x = x_ref[...]
    row = lax.broadcasted_iota(jnp.int32, (members * seq, rows + seq), 0)
    lane = lax.broadcasted_iota(jnp.int32, (members * seq, rows + seq), 1)
    own = (row // seq) == (lane // R)
    pick = (lane - rows) == (row % seq)
    for s in range(2):
        noise = own_noise(seeds_ref, 2 * s, hashes, depth)
        padded = jnp.concatenate([noise, jnp.zeros((seq, depth), jnp.bfloat16)], axis=0)
        coeff = lax.dot_general(x, padded, MINOR, preferred_element_type=jnp.float32) * scale
        tiled = jnp.concatenate([coeff] * members, axis=0)
        out_ref[s] = jnp.where(
            lane < rows, jnp.where(own, tiled, 0.0), jnp.where(pick, 1.0, 0.0)
        ).astype(jnp.bfloat16)


def left_operands(seeds, inputs, base, info):
    seq = inputs.shape[0]
    members = seeds.shape[0]
    return pl.pallas_call(
        coeff_kernel,
        out_shape=(
            jax.ShapeDtypeStruct((2, members * seq, members * R + seq), jnp.bfloat16),
            jax.ShapeDtypeStruct((2,) + base.shape, base.dtype),
            jax.ShapeDtypeStruct(info.shape, info.dtype),
        ),
        in_specs=[SCALARS, WHOLE, WHOLE, WHOLE],
        out_specs=(WHOLE, WHOLE, WHOLE),
        compiler_params=room(12),
        cost_estimate=pl.CostEstimate(flops=10**7, bytes_accessed=10**6, transcendentals=0),
        name="coeff",
    )(seeds, inputs, base, info)


def noise_kernel(seeds_ref, out_ref, hash_ref, *, part, population):
    tiles, width = hash_ref.shape[:2]
    rows = width // 9
    offset = lax.axis_index("pop") * width

    def fill(r, carry):
        column = lax.broadcasted_iota(jnp.int32, (rows, 128), 0) + (offset + r * rows)
        lane = lax.broadcasted_iota(jnp.int32, (rows, 128), 1)
        for t in range(tiles):
            hash_ref[t, pl.ds(pl.multiple_of(r * rows, 8), rows), :] = mixed(
                column * R + (lane + 128 * t) // population + 1
            )
        return carry

    lax.fori_loop(0, 9, fill, 0)
    for start in range(0, out_ref.shape[2], part):
        hashes = entries(start, 8, part)
        for s in range(2):
            out_ref[s, :, start : start + part] = own_noise(seeds_ref, 2 * s + 1, hashes, part)


def output_noise(seeds, total, width, population):
    return pl.pallas_call(
        functools.partial(noise_kernel, part=1536, population=population),
        out_shape=(
            jax.ShapeDtypeStruct((2, seeds.shape[0] * R, total), jnp.bfloat16),
            jax.ShapeDtypeStruct((population * R // 128, width, 128), jnp.int32),
        ),
        in_specs=[SCALARS],
        out_specs=(WHOLE, WHOLE),
        compiler_params=room(8),
        cost_estimate=pl.CostEstimate(flops=10**7, bytes_accessed=10**6, transcendentals=0),
        name="noise",
    )(seeds)


def chip_at(place, chips):
    if chips <= 8:
        return jnp.where(place < chips // 2, 2 * place, 2 * (chips - 1 - place) + 1)
    return place


def ring_place(chip, chips):
    if chips <= 8:
        return jnp.where(chip % 2 == 0, chip // 2, chips - 1 - chip // 2)
    return chip


def hidden_kernel(left_ref, noise_ref, *rest, seq, sub, chunk):
    shard_refs, (out_ref, ordered, base, buf, sems) = rest[:-5], rest[-5:]
    chips = len(shard_refs)
    reach = chips // 2
    width = base.shape[1] // (2 * chips)
    group = 128 // math.gcd(width, 128)
    position = lax.axis_index("pop")
    core = lax.rem(position, 2)
    here = ring_place(position // 2, chips)
    for i, ref in enumerate(shard_refs):
        step = i if i <= reach else i - reach
        toward = 2 * core - 1 if i <= reach else 1 - 2 * core
        chip = chip_at(lax.rem(here + toward * step + chips, chips), chips)
        owner = core if i <= reach else 1 - core
        for c in range(2):
            ordered[2 * chip + (owner if c == 0 else 1 - owner)] = ref[c]
    for first in range(0, 2 * chips, group):
        base[:, first * width : (first + group) * width] = jnp.concatenate(
            [ordered[shard] for shard in range(first, first + group)], axis=1
        )
    copies = []
    for begin in range(0, out_ref.shape[1], sub):
        part = slice(begin, begin + sub)
        totals = []
        for s in range(2):
            right = jnp.concatenate(
                [noise_ref[s, :, part], base[s * seq : (s + 1) * seq, part]], axis=0
            )
            totals.append(jnp.dot(left_ref[s], right, preferred_element_type=jnp.float32))
        half = 0.5 * totals[0]
        buf[:, part] = ((half + half * jnp.tanh(half)) * totals[1]).astype(jnp.bfloat16)
        if (begin + sub) % chunk == 0:
            i = begin // chunk
            span = pl.ds(i * chunk, chunk)
            copies.append(
                pltpu.make_async_copy(buf.at[:, span], out_ref.at[:, span], sems.at[i])
            )
            copies[-1].start()
    for copy in copies:
        copy.wait()


def hidden_states(left, noise, shards, width, seq, sub=256, chunk=1536):
    rows = left.shape[1]
    total = noise.shape[2]
    return pl.pallas_call(
        functools.partial(hidden_kernel, seq=seq, sub=sub, chunk=chunk),
        out_shape=jax.ShapeDtypeStruct((rows, total), jnp.bfloat16),
        in_specs=[WHOLE] * (2 + len(shards)),
        out_specs=PLACED,
        scratch_shapes=[
            pltpu.VMEM((2 * len(shards), 2 * seq, width), jnp.bfloat16),
            pltpu.VMEM((2 * seq, total), jnp.bfloat16),
            pltpu.VMEM((rows, total), jnp.bfloat16),
            pltpu.SemaphoreType.DMA((total // chunk,)),
        ],
        compiler_params=room(16),
        cost_estimate=pl.CostEstimate(
            flops=10**8, bytes_accessed=6 * 10**6, transcendentals=2 * 10**6
        ),
        name="hidden",
    )(left, noise, *shards)


def columns_kernel(info_ref, got_ref, hash_ref, cols_ref, keys_ref, *, population):
    width, terms = cols_ref.shape[1:]
    norm = NOISE_SCALE * NOISE_SCALE / math.sqrt(population * R)
    info = info_ref[...] + got_ref[...]
    seeds = info[0:1, 0:population]
    ranks = info[1:2, 0:population]
    scale = ((ranks.astype(jnp.float32) + 0.5) / population - 0.5) * norm
    scales = jnp.concatenate([scale] * R, axis=1)
    wide = jnp.concatenate([seeds] * R, axis=1)
    for s in range(2):
        for t in range(0, population, 64):
            square = jnp.broadcast_to(seeds[:, t : t + 64].astype(jnp.float32), (128, 64))
            keys_ref[s, t : t + 64, :] = mixed(square.T.astype(jnp.int32) * 4 + 2 * s)
    lane_keys = [mixed(wide * 4 + (2 * s + 1)) for s in range(2)]
    part = width // 9

    def fill(r, carry):
        where = pl.ds(pl.multiple_of(r * part, 8), part)
        for t in range(0, terms, 128):
            hashes = hash_ref[t // 128, where, :]
            for s in range(2):
                noise = centered(hashes ^ lane_keys[s][:, t : t + 128])
                cols_ref[s, where, t : t + 128] = (noise * scales[:, t : t + 128]).astype(jnp.bfloat16)
        return carry

    lax.fori_loop(0, 9, fill, 0)


def update_columns(info, got, hashes, population, width):
    return pl.pallas_call(
        functools.partial(columns_kernel, population=population),
        out_shape=(
            jax.ShapeDtypeStruct((2, width, population * R), jnp.bfloat16),
            jax.ShapeDtypeStruct((2, population, 128), jnp.int32),
        ),
        in_specs=[WHOLE, WHOLE, WHOLE],
        out_specs=(WHOLE, WHOLE),
        compiler_params=room(8),
        cost_estimate=pl.CostEstimate(flops=10**7, bytes_accessed=10**6, transcendentals=0),
        name="columns",
    )(info, got, hashes)


def update_kernel(keys_ref, cols_ref, out_ref, buf, rows_buf, sems, *, stream, sub, chunk):
    depth = out_ref.shape[1]
    population = keys_ref.shape[1]

    def generate(j):
        hashes = entries(j * sub, 8, sub)
        slot = j % 2
        for k in range(R):
            for q in range(0, sub, 128):
                entry = jnp.broadcast_to(hashes[k : k + 1, q : q + 128], (16, 128))
                for t in range(0, population, 16):
                    at = k * population + t
                    rows_buf[slot, at : at + 16, q : q + 128] = centered(
                        entry ^ keys_ref[stream, t : t + 16, :]
                    ).astype(jnp.bfloat16)

    count = depth // sub
    copies = []
    generate(0)
    for j in range(count):
        if j + 1 < count:
            generate(j + 1)
        buf[:, j * sub : (j + 1) * sub] = jnp.dot(
            cols_ref[stream], rows_buf[j % 2], preferred_element_type=jnp.float32
        ).astype(jnp.bfloat16)
        if (j + 1) * sub % chunk == 0:
            i = j * sub // chunk
            span = pl.ds(i * chunk, chunk)
            copies.append(
                pltpu.make_async_copy(buf.at[:, span], out_ref.at[:, span], sems.at[i])
            )
            copies[-1].start()
    for copy in copies:
        copy.wait()


def update(keys, cols, stream, depth, sub=256, chunk=512):
    width, terms = cols.shape[1:]
    return pl.pallas_call(
        functools.partial(update_kernel, stream=stream, sub=sub, chunk=chunk),
        out_shape=jax.ShapeDtypeStruct((width, depth), jnp.bfloat16),
        in_specs=[WHOLE, WHOLE],
        out_specs=PLACED,
        scratch_shapes=[
            pltpu.VMEM((width, depth), jnp.bfloat16),
            pltpu.VMEM((2, terms, sub), jnp.bfloat16),
            pltpu.SemaphoreType.DMA((depth // chunk,)),
        ],
        compiler_params=room(24),
        cost_estimate=pl.CostEstimate(
            flops=2 * width * terms * depth, bytes_accessed=2 * width * depth, transcendentals=0
        ),
        name="update",
    )(keys, cols)


def ring_order(chips):
    if chips <= 8:
        return list(range(0, chips, 2)) + list(range(chips - 1, 0, -2))
    return list(range(chips))


def together(*values):
    return lax.optimization_barrier(values)


def per_device(inputs, gate_weight, up_weight, member_seeds, member_ranks):
    devices = lax.axis_size("pop")
    depth, width = gate_weight.shape
    local = member_seeds.shape[0]
    seq = inputs.shape[0]
    population = devices * local
    chips = devices // 2
    order = ring_order(chips)
    siblings = [(i, i ^ 1) for i in range(devices)]
    onward = [
        (2 * order[i] + c, 2 * order[(i + 1 - 2 * c) % chips] + c) for i in range(chips) for c in range(2)
    ]

    base, info = base_projections(
        member_seeds, member_ranks, inputs, gate_weight.T, up_weight.T, -(-population // 128) * 128
    )

    def named(value, pairs):
        return lax.ppermute(value, "pop", pairs)

    def seed_step(info, stride):
        return named(info, [(i, i ^ stride) for i in range(devices)])

    got = seed_step(info, 1)
    sibling = lax.ppermute(base, "pop", siblings)
    left, pair, info = left_operands(member_seeds, inputs, base, info)
    info, pair, sibling, left = together(info + got, pair, sibling, left)
    stride = 2
    got = seed_step(info, stride)
    moving = lax.dynamic_update_slice(pair, sibling[None], (1, 0, 0))
    arrived, crossed = [moving], []
    noise, hashes = output_noise(
        together(member_seeds, moving)[0], devices * width, width, population
    )
    cols = keys = None
    updates = [None, None]
    for k in range(1, chips // 2 + 1):
        onto = named(moving, onward)
        if k == 1:
            onto, noise = together(onto, noise)
        else:
            crossed.append(lax.ppermute(moving, "pop", siblings))
        if cols is None and 2 * stride < devices:
            info = info + got
            stride *= 2
            got = seed_step(info, stride)
        elif cols is None:
            cols, keys = update_columns(
                *together(info, got, moving)[:2], hashes, population, width
            )
            updates[0] = update(keys, cols, 0, depth)
            onto, cols, first = together(onto, cols, updates[0])
            updates[0] = first
        elif updates[1] is None:
            updates[1] = update(keys, cols, 1, depth)
        moving = onto
        arrived.append(moving)
    noise = together(noise, *updates)[0]
    hidden = hidden_states(left, noise, arrived + crossed, width, seq)
    return (hidden.reshape(local, seq, -1), updates[0].T, updates[1].T)


def solution(mesh):
    placed = (P("grp", None), P(None, "pop"), P(None, "pop"), P(("grp", "pop")), P(("grp", "pop")))
    return jax.shard_map(
        per_device,
        mesh=mesh,
        in_specs=placed,
        out_specs=(P(("grp", "pop"), None, None), P("grp", "pop"), P("grp", "pop")),
        check_vma=False,
    )
```
